256 devices in a mesh: tm: 32 (over z, y), fsdp: 8 (over x, core).
Axes of the slice: x: 4, y: 4, z: 8, core: 2. Of those that a mesh axis runs over, the one named last changes fastest.
Arguments:
- inputs: bfloat16 [8, 8192, 2048], P('fsdp', 'tm'), may hold values from -6 to 6
- query_rows: bfloat16 [8, 8192, 1024], P('fsdp', 'tm'), may hold values from -8 to 8
- saved_key_rows: bfloat16 [8, 8192, 1024], P('fsdp', 'tm'), may hold values from -8 to 8
- value_rows: bfloat16 [8, 8192, 1024], P('fsdp', 'tm'), may hold values from -6 to 6
- grad_out: bfloat16 [8, 8192, 1024], P('fsdp', 'tm'), may hold values from -24 to 24
- key_weight: bfloat16 [2048, 1024], P('fsdp'), may hold values from -0.125 to 0.125
- value_weight: bfloat16 [2048, 1024], P('fsdp'), may hold values from -0.125 to 0.125
- block_pairs: int32 [32, 8, 2], P('tm'), may hold values from 0 to 63, as said below
- pair_counts: int32 [32], P('tm'), may hold values from 2 to 8, as said below
Outputs:
- grad_query: bfloat16 [8, 8192, 1024], P('fsdp', 'tm')
- input_gradient_rows: bfloat16 [8, 8192, 2048], P('fsdp', 'tm')
- grad_key_weight: float32 [2048, 1024], P('fsdp', 'tm')
- grad_value_weight: float32 [2048, 1024], P('fsdp', 'tm')
The draws below stay inside these ranges and needn't reach their ends.
Inputs may be any that keep to these rules, and one draw needn't show every extreme that they name: `block_pairs`: row r of shard j names (query block, key block) by block numbers along the sequence. The first pair_counts[j] rows are shard j's part of the mask: the query block is one of shard j's 2 blocks, the key block is at most the query block and above the query block minus 4, no pair stands twice, and each of the shard's query blocks is paired with itself. Rows from pair_counts[j] on are not part of the mask. `pair_counts`: some shard holds all 8 pairs of its band in every draw.
All inputs are finite; a program needn't handle non-finite values.
Results may differ from the reference program's by a relative error of at most 0.012.
Values may be sent and summed in bfloat16 or wider, within the bound.
A program may use at most 128 MiB of HBM per device.

```python
import jax
import jax.numpy as jnp
from jax import lax

D = 2048
H = 8
HS = 128
BLK = 128
WB = 4
TOK_DEV = 256
HD = 1024
QBD = 2
REACH = 2
MAXP = 8
L = 8192
SEQS = 8
N_TM = 32


def draw_query_rows(key, part):
    values = jnp.clip(jax.random.normal(jax.random.fold_in(key, 3), (SEQS, L, HD), jnp.float32), -6.0, 6.0)
    return values.astype(jnp.bfloat16)


def draw_saved_key_rows(key, part):
    values = jnp.clip(jax.random.normal(jax.random.fold_in(key, 5), (SEQS, L, HD), jnp.float32), -6.0, 6.0)
    return values.astype(jnp.bfloat16)


def mask_tables(key):
    base = jax.random.fold_in(key, 29)
    shard_ids = jnp.arange(N_TM)[:, None]
    slot_ids = jnp.arange(MAXP)[None, :]
    query_block = shard_ids * QBD + slot_ids // WB
    key_block = query_block - slot_ids % WB
    row_boundaries = jax.random.randint(jax.random.fold_in(base, 1), (N_TM, 1), 10, 101)
    dense_shard = jax.random.randint(jax.random.fold_in(base, 2), (), REACH, N_TM)
    row_boundaries = jnp.where(shard_ids == dense_shard, 101, row_boundaries)
    rolls = jax.random.randint(jax.random.fold_in(base, 3), (N_TM, MAXP), 0, 100)
    kept = (slot_ids % WB == 0) | (key_block >= 0) & (rolls < row_boundaries)
    ranking = jnp.where(kept, 0, MAXP) + slot_ids
    ordering = jnp.argsort(ranking, axis=1)
    listed = jnp.stack((query_block, jnp.maximum(key_block, 0)), axis=2)
    listed = jnp.take_along_axis(listed, ordering[:, :, None], axis=1)
    totals = jnp.sum(kept.astype(jnp.int32), axis=1)
    return (listed.astype(jnp.int32), totals.astype(jnp.int32))


def draw_block_pairs(key, part):
    listed, totals = mask_tables(key)
    return listed


def draw_pair_counts(key, part):
    listed, totals = mask_tables(key)
    return totals


def steps_of(stream_key, dims, pieces, low, high):
    def one(axis_at, shards_of):
        steps = jax.random.uniform(jax.random.fold_in(jax.random.fold_in(stream_key, 6), axis_at), (shards_of,), jnp.float32, low / len(pieces), high / len(pieces))
        return jnp.repeat(jnp.exp(steps), dims[axis_at] // shards_of).reshape((-1,) + (1,) * (len(dims) - axis_at - 1))

    loudness = one(*pieces[0])
    for cut in pieces[1:]:
        loudness = loudness * one(*cut)
    return loudness


def bell_draw(key, shape, deviation, most, split=(), kind=jnp.bfloat16):
    entries = deviation * jax.random.normal(key, shape, jnp.float32)
    if split:
        entries = entries * steps_of(key, shape, split, -0.22, 0.18)
    return jnp.clip(entries, -most, most).astype(kind)


def setup_inputs(seed: int = 0) -> dict:
    keys = jax.random.split(jax.random.key(seed), 10)
    inputs = bell_draw(keys[0], (SEQS, L, D), 1.0, 6.0, ((0, 8), (1, 32)))
    query_rows = draw_query_rows(jax.random.fold_in(keys[9], 71), 0)
    saved_key_rows = draw_saved_key_rows(jax.random.fold_in(keys[9], 71), 0)
    value_rows = bell_draw(keys[3], (SEQS, L, HD), 1.0, 6.0, ((0, 8), (1, 32)))
    grad_out = bell_draw(keys[4], (SEQS, L, HD), 4.0, 24.0, ((0, 8), (1, 32)))
    key_weight = bell_draw(keys[5], (D, HD), D ** -0.5, 0.125, ((0, 8),))
    value_weight = bell_draw(keys[6], (D, HD), D ** -0.5, 0.125, ((0, 8),))
    block_pairs = draw_block_pairs(jax.random.fold_in(keys[9], 71), 0)
    pair_counts = draw_pair_counts(jax.random.fold_in(keys[9], 71), 0)
    return {"inputs": inputs, "query_rows": query_rows, "saved_key_rows": saved_key_rows, "value_rows": value_rows, "grad_out": grad_out, "key_weight": key_weight, "value_weight": value_weight, "block_pairs": block_pairs, "pair_counts": pair_counts}


def head_terms(allowed, query_head, key_head, value_head, cotangent_head):
    score_scale = query_head.shape[-1] ** -0.5
    query_wide = query_head.astype(jnp.float32)
    key_wide = key_head.astype(jnp.float32)
    value_wide = value_head.astype(jnp.float32)
    cotangent_wide = cotangent_head.astype(jnp.float32)
    scores = jnp.einsum("qd,kd->qk", query_wide, key_wide) * score_scale
    scores = jnp.where(allowed, scores, -jnp.inf)
    largest = jnp.max(scores, axis=1, keepdims=True)
    weights = jnp.exp(scores - largest)
    weights = weights / jnp.sum(weights, axis=1, keepdims=True)
    weights_low = weights.astype(jnp.bfloat16)
    weights_back = weights_low.astype(jnp.float32)
    attended = jnp.einsum("qk,kd->qd", weights_back, value_wide)
    row_dot = jnp.sum(cotangent_wide * attended, axis=1, keepdims=True)
    grad_probs = jnp.einsum("qd,kd->qk", cotangent_wide, value_wide)
    grad_low = (weights * (grad_probs - row_dot)).astype(jnp.bfloat16)
    grad_back = grad_low.astype(jnp.float32)
    grad_q = jnp.einsum("qk,kd->qd", grad_back, key_wide) * score_scale
    grad_k = jnp.einsum("qk,qd->kd", grad_back, query_wide) * score_scale
    grad_v = jnp.einsum("qk,qd->kd", weights_back, cotangent_wide)
    return grad_q, grad_k, grad_v


def split_heads(array):
    return jnp.transpose(array.reshape(array.shape[0], H, HS), (1, 0, 2))


def join_heads(array):
    return jnp.transpose(array, (1, 0, 2)).reshape(array.shape[1], H * HS)


def reference(inputs, query_rows, saved_key_rows, value_rows, grad_out, key_weight, value_weight, block_pairs, pair_counts):
    window_len = (REACH + 1) * TOK_DEV
    nblocks = L // BLK
    is_valid = (jnp.arange(MAXP)[None, :] < pair_counts[:, None]).astype(jnp.int32)
    block_table = jnp.zeros((nblocks, nblocks), jnp.int32)
    block_table = block_table.at[block_pairs[:, :, 0].reshape(-1), block_pairs[:, :, 1].reshape(-1)].max(is_valid.reshape(-1))
    block_table = jnp.concatenate((jnp.zeros((nblocks, REACH * QBD), jnp.int32), block_table), axis=1)

    def sequence_grads(operands):
        query_seq, key_seq, value_seq, cotangent_seq = operands
        front = jnp.zeros((REACH * TOK_DEV, HD), key_seq.dtype)
        key_pad = jnp.concatenate((front, key_seq), axis=0)
        value_pad = jnp.concatenate((front, value_seq), axis=0)

        def shard_grads(shard_id):
            row_start = shard_id * TOK_DEV
            query_portion = lax.dynamic_slice_in_dim(query_seq, row_start, TOK_DEV, 0)
            cotangent_part = lax.dynamic_slice_in_dim(cotangent_seq, row_start, TOK_DEV, 0)
            key_window = lax.dynamic_slice_in_dim(key_pad, row_start, window_len, 0)
            value_window = lax.dynamic_slice_in_dim(value_pad, row_start, window_len, 0)
            block_allowed = lax.dynamic_slice(block_table, (shard_id * QBD, shard_id * QBD), (QBD, (REACH + 1) * QBD)) > 0
            tile_allowed = jnp.repeat(jnp.repeat(block_allowed, BLK, axis=0), BLK, axis=1)
            query_pos = row_start + jnp.arange(TOK_DEV, dtype=jnp.int32)
            key_pos = row_start - REACH * TOK_DEV + jnp.arange(window_len, dtype=jnp.int32)
            allowed = tile_allowed & (key_pos[None, :] <= query_pos[:, None])

            def per_head(head_ops):
                return head_terms(allowed, head_ops[0], head_ops[1], head_ops[2], head_ops[3])

            head_q, head_k, head_v = lax.map(per_head, (split_heads(query_portion), split_heads(key_window), split_heads(value_window), split_heads(cotangent_part)))
            return join_heads(head_q).astype(jnp.bfloat16), join_heads(head_k), join_heads(head_v)

        shard_q, shard_k, shard_v = lax.map(shard_grads, jnp.arange(N_TM, dtype=jnp.int32))
        grad_keys = shard_k[:, REACH * TOK_DEV:, :]
        grad_values = shard_v[:, REACH * TOK_DEV:, :]
        for offset in range(1, REACH + 1):
            lowest_row_index = (REACH - offset) * TOK_DEV
            padding_values = jnp.zeros((offset, TOK_DEV, HD), jnp.float32)
            piece_k = shard_k[:, lowest_row_index:lowest_row_index + TOK_DEV, :]
            piece_v = shard_v[:, lowest_row_index:lowest_row_index + TOK_DEV, :]
            grad_keys = grad_keys + jnp.concatenate((piece_k[offset:], padding_values), axis=0)
            grad_values = grad_values + jnp.concatenate((piece_v[offset:], padding_values), axis=0)
        return shard_q.reshape(L, HD), grad_keys.reshape(L, HD), grad_values.reshape(L, HD)

    grad_query, grad_keys, grad_values = lax.map(sequence_grads, (query_rows, saved_key_rows, value_rows, grad_out))
    paired_lower_rows = jnp.concatenate((grad_keys.astype(jnp.bfloat16), grad_values.astype(jnp.bfloat16)), axis=2)
    paired_weight_matrices = jnp.concatenate((key_weight, value_weight), axis=1).astype(jnp.float32)
    input_gradient_rows = jnp.einsum("ixn,kn->ixk", paired_lower_rows.astype(jnp.float32), paired_weight_matrices).astype(jnp.bfloat16)
    shaped_inputs = jnp.transpose(inputs.reshape(SEQS, N_TM, TOK_DEV, D), (1, 0, 2, 3))
    shaped_grads = jnp.transpose(paired_lower_rows.reshape(SEQS, N_TM, TOK_DEV, 2 * HD), (1, 0, 2, 3))

    def shard_weights(total, operands):
        input_shard, grad_shard = operands
        partials = jnp.einsum("std,stc->sdc", input_shard.astype(jnp.float32), grad_shard.astype(jnp.float32))
        return total + jnp.sum(partials, axis=0), None

    weight_grads, unused = lax.scan(shard_weights, jnp.zeros((D, 2 * HD), jnp.float32), (shaped_inputs, shaped_grads))
    return (grad_query, input_gradient_rows, weight_grads[:, :HD], weight_grads[:, HD:])
```

```python
import jax
import jax.numpy as jnp
from jax import lax
from jax.experimental import pallas as pl
from jax.experimental.pallas import tpu as pltpu
from jax.sharding import PartitionSpec as P

H = 8
HS = 128
BLK = 128
HD = 1024
QBD = 2
REACH = 2
MAXP = 8


def from_behind(value, axis, steps):
    count = lax.axis_size(axis)
    leading, last = (max(0, -steps), min(count, count - steps))
    return lax.ppermute(value, axis, [(source, source + steps) for source in range(leading, last)])


def head_terms(allowed, query_head, key_head, value_head, cotangent_head):
    score_scale = query_head.shape[-1] ** (-0.5)
    scores = (
        jnp.einsum("qd,kd->qk", query_head, key_head, preferred_element_type=jnp.float32)
        * score_scale
    )
    scores = jnp.where(allowed, scores, -jnp.inf)
    largest = jnp.max(scores, axis=1, keepdims=True)
    weights = jnp.exp(scores - largest)
    weights = weights / jnp.sum(weights, axis=1, keepdims=True)
    weights_low = weights.astype(jnp.bfloat16)
    attended = jnp.dot(weights_low, value_head, preferred_element_type=jnp.float32)
    row_dot = jnp.sum(cotangent_head.astype(jnp.float32) * attended, axis=1, keepdims=True)
    grad_probs = jnp.einsum(
        "qd,kd->qk", cotangent_head, value_head, preferred_element_type=jnp.float32
    )
    grad_low = (weights * (grad_probs - row_dot)).astype(jnp.bfloat16)
    grad_q = jnp.dot(grad_low, key_head, preferred_element_type=jnp.float32) * score_scale
    grad_k = (
        jnp.einsum("qk,qd->kd", grad_low, query_head, preferred_element_type=jnp.float32)
        * score_scale
    )
    grad_v = jnp.einsum(
        "qk,qd->kd", weights_low, cotangent_head, preferred_element_type=jnp.float32
    )
    return (grad_q, grad_k, grad_v)


def split_heads(array):
    return jnp.transpose(array.reshape(array.shape[0], H, HS), (1, 0, 2))


def join_heads(array):
    return jnp.transpose(array, (1, 0, 2)).reshape(array.shape[1], H * HS)


def shards(
    inputs,
    query_rows,
    saved_key_rows,
    value_rows,
    grad_out,
    key_weight,
    value_weight,
    block_pairs,
    pair_counts,
):
    tokens = query_rows.shape[1]
    shard_id = lax.axis_index("tm")
    key_local = saved_key_rows[0]
    value_local = value_rows[0]
    panels = [(key_local, value_local)]
    for offset in range(1, REACH + 1):
        panels.append(from_behind((key_local, value_local), "tm", offset))
    window_keys = jnp.concatenate([panels[offset][0] for offset in range(REACH, -1, -1)], axis=0)
    window_values = jnp.concatenate([panels[offset][1] for offset in range(REACH, -1, -1)], axis=0)
    window_len = (REACH + 1) * tokens
    is_valid = jnp.arange(MAXP) < pair_counts[0]
    query_blocks = shard_id * QBD + jnp.arange(QBD, dtype=jnp.int32)
    key_blocks = (shard_id - REACH) * QBD + jnp.arange((REACH + 1) * QBD, dtype=jnp.int32)
    pair_hits = (
        is_valid[:, None, None]
        & (block_pairs[0, :, 0][:, None, None] == query_blocks[None, :, None])
        & (block_pairs[0, :, 1][:, None, None] == key_blocks[None, None, :])
    )
    block_allowed = jnp.any(pair_hits, axis=0)
    tile_allowed = jnp.repeat(jnp.repeat(block_allowed, BLK, axis=0), BLK, axis=1)
    query_pos = shard_id * tokens + jnp.arange(tokens, dtype=jnp.int32)
    key_pos = (shard_id - REACH) * tokens + jnp.arange(window_len, dtype=jnp.int32)
    allowed = tile_allowed & (key_pos[None, :] <= query_pos[:, None])

    def per_head(head_ops):
        return head_terms(allowed, head_ops[0], head_ops[1], head_ops[2], head_ops[3])

    head_q, head_k, head_v = lax.map(
        per_head,
        (
            split_heads(query_rows[0]),
            split_heads(window_keys),
            split_heads(window_values),
            split_heads(grad_out[0]),
        ),
    )
    grad_query = join_heads(head_q).astype(jnp.bfloat16)[None]
    key_window = join_heads(head_k)
    value_window = join_heads(head_v)

    def key_piece(offset):
        return key_window[(REACH - offset) * tokens : (REACH - offset + 1) * tokens]

    def value_piece(offset):
        return value_window[(REACH - offset) * tokens : (REACH - offset + 1) * tokens]

    grad_keys = key_piece(0)
    grad_values = value_piece(0)
    for offset in range(1, REACH + 1):
        returned = from_behind((key_piece(offset), value_piece(offset)), "tm", -offset)
        grad_keys = grad_keys + returned[0]
        grad_values = grad_values + returned[1]
    keys_low = grad_keys.astype(jnp.bfloat16)
    values_low = grad_values.astype(jnp.bfloat16)
    paired_lower_rows = jnp.concatenate((keys_low, values_low), axis=1)
    pieces = lax.all_gather((key_weight, value_weight), "fsdp", axis=0, tiled=True)
    key_part = jnp.einsum("tc,rc->tr", keys_low, pieces[0], preferred_element_type=jnp.float32)
    value_part = jnp.einsum("tc,rc->tr", values_low, pieces[1], preferred_element_type=jnp.float32)
    input_gradient_rows = (key_part + value_part).astype(jnp.bfloat16)[None]
    key_total, value_total = weight_grads(inputs[0], paired_lower_rows)
    return (grad_query, input_gradient_rows, key_total, value_total)


BF = jnp.bfloat16
F32 = jnp.float32
MESH = pl.DeviceIdType.MESH
RING = 4
NZ = 8
TILE = 256


class Place:
    def __init__(self):
        tm = lax.axis_index("tm")
        fsdp = lax.axis_index("fsdp")
        self.z, self.y = tm // RING, tm % RING
        self.x, self.core = fsdp // 2, fsdp % 2

    def at(self, x=None, core=None, z=None, y=None):
        x = self.x if x is None else x
        core = self.core if core is None else core
        z = self.z if z is None else z
        y = self.y if y is None else y
        return (z * RING + y, x * 2 + core)

    def step(self, axis, by):
        if axis == "x":
            return self.at(x=(self.x + by) % RING)
        if axis == "y":
            return self.at(y=(self.y + by) % RING)
        return self.at(z=(self.z + by) % NZ)

    def partner(self):
        return self.at(core=1 - self.core)


def greet(devices):
    barrier = pltpu.get_barrier_semaphore()
    for device in devices:
        pl.semaphore_signal(barrier, inc=1, device_id=device, device_id_type=MESH)
    pl.semaphore_wait(barrier, len(devices))


def weight_kernel(
    x_ref,
    g_ref,
    key_ref,
    value_ref,
    gt,
    xs,
    opp_send,
    opp_recv,
    nb_send,
    nb_recv,
    opp2_send,
    opp2_recv,
    nb2_send,
    nb2_recv,
    sums,
    final,
    z_send,
    z_recv,
    core_sems,
    ring_sems,
    z_sems,
):
    here = Place()
    greet(
        [here.partner()]
        + [here.step(axis, by) for axis in ("x", "y") for by in (1, 3)]
        + [here.step("z", by) for by in range(1, NZ)]
    )
    sent = []

    def send(src, dst, sems, at, device):
        copy = pltpu.make_async_remote_copy(
            src_ref=src,
            dst_ref=dst,
            send_sem=sems.at[(0,) + at],
            recv_sem=sems.at[(1,) + at],
            device_id=device,
            device_id_type=MESH,
        )
        copy.start()
        sent.append(copy)
        return copy

    crossing = []
    for xp in range(RING):
        theirs = pl.multiple_of(xp * 512 + (1 - here.core) * TILE, TILE)
        crossing.append(
            send(
                x_ref.at[:, pl.ds(theirs, TILE)],
                xs.at[1, xp],
                core_sems,
                (xp,),
                here.partner(),
            )
        )
    for half in range(2):
        for zp in range(NZ):
            first = half * HD + zp * 128
            turned = g_ref[:, first : first + 128].T
            for yp in range(RING):
                gt[0, half, yp, zp * 32 : zp * 32 + 32, :] = turned[yp * 32 : yp * 32 + 32]
        crossing.append(
            send(gt.at[0, half], gt.at[1, half], core_sems, (RING + half,), here.partner())
        )
    for xp in range(RING):
        mine = pl.multiple_of(xp * 512 + here.core * TILE, TILE)
        xs[0, xp] = x_ref[:, pl.ds(mine, TILE)]
    for copy in crossing:
        copy.wait_recv()

    axes = (("x", "y"), ("y", "x"))
    place = {"x": here.x, "y": here.y}

    def block(t, ring, b):
        xp, yp = (ring, b) if t == 0 else (b, ring)
        return jnp.dot(gt[0, t, yp], xs[0, xp], preferred_element_type=F32) + jnp.dot(
            gt[1, t, yp], xs[1, xp], preferred_element_type=F32
        )

    first, pieces = [], []
    for t in range(2):
        axis = axes[t][0]
        opp = (place[axis] + 2) % RING
        for b in range(4):
            opp_send[t, b] = block(t, opp, b).astype(BF)
        first.append(
            [
                send(
                    opp_send.at[t, pl.ds(2 * d, 2)],
                    opp_recv.at[t, d],
                    ring_sems,
                    (t, d),
                    here.step(axis, (1, 3)[d]),
                )
                for d in range(2)
            ]
        )
    for t in range(2):
        axis = axes[t][0]
        for d in range(2):
            ring = (place[axis] + (1, 3)[d]) % RING
            lo = (2, 0)[d]
            for b in (lo, lo + 1):
                nb_send[t, d, b] = block(t, ring, b).astype(BF)
            pieces.append(
                send(
                    nb_send.at[t, d, pl.ds(lo, 2)],
                    nb_recv.at[t, d, pl.ds(lo, 2)],
                    ring_sems,
                    (t, 2 + d),
                    here.step(axis, (1, 3)[d]),
                )
            )
    for t in range(2):
        axis = axes[t][0]
        for d in range(2):
            ring = (place[axis] + (1, 3)[d]) % RING
            lo = (0, 2)[d]
            first[t][d].wait_recv()
            for b in (lo, lo + 1):
                nb_send[t, d, b] = (
                    block(t, ring, b) + opp_recv[t, d, b - lo].astype(F32)
                ).astype(BF)
            pieces.append(
                send(
                    nb_send.at[t, d, pl.ds(lo, 2)],
                    nb_recv.at[t, d, pl.ds(lo, 2)],
                    ring_sems,
                    (t, 4 + d),
                    here.step(axis, (1, 3)[d]),
                )
            )
    for copy in pieces:
        copy.wait_recv()

    second = []
    for t in range(2):
        axis1, axis2 = axes[t]

        def total(b):
            return (
                block(t, place[axis1], b)
                + nb_recv[t, 0, b].astype(F32)
                + nb_recv[t, 1, b].astype(F32)
            )

        opp2_send[t] = total((place[axis2] + 2) % RING).astype(BF)
        second.append(
            [
                send(
                    opp2_send.at[t, pl.ds(128 * d, 128)],
                    opp2_recv.at[t, d],
                    ring_sems,
                    (t, 6 + d),
                    here.step(axis2, (1, 3)[d]),
                )
                for d in range(2)
            ]
        )
        for d in range(2):
            sums[t, d] = total((place[axis2] + (1, 3)[d]) % RING)
        sums[t, 2] = total(place[axis2])
    pieces = []
    for t in range(2):
        for d in range(2):
            lo = (128, 0)[d]
            nb2_send[t, d, lo : lo + 128] = sums[t, d, lo : lo + 128].astype(BF)
            pieces.append(
                send(
                    nb2_send.at[t, d, pl.ds(lo, 128)],
                    nb2_recv.at[t, d, pl.ds(lo, 128)],
                    ring_sems,
                    (t, 8 + d),
                    here.step(axes[t][1], (1, 3)[d]),
                )
            )
    for t in range(2):
        for d in range(2):
            lo = (0, 128)[d]
            second[t][d].wait_recv()
            nb2_send[t, d, lo : lo + 128] = (
                sums[t, d, lo : lo + 128] + opp2_recv[t, d].astype(F32)
            ).astype(BF)
            pieces.append(
                send(
                    nb2_send.at[t, d, pl.ds(lo, 128)],
                    nb2_recv.at[t, d, pl.ds(lo, 128)],
                    ring_sems,
                    (t, 10 + d),
                    here.step(axes[t][1], (1, 3)[d]),
                )
            )
    for copy in pieces:
        copy.wait_recv()
    for t in range(2):
        whole = sums[t, 2] + nb2_recv[t, 0].astype(F32) + nb2_recv[t, 1].astype(F32)
        for zp in range(NZ):
            part = whole[zp * 32 : zp * 32 + 32]
            final[zp, t] = part
            z_send[zp, t] = part.astype(BF)
    pieces = []
    for by in range(1, NZ):
        pieces.append(
            send(
                z_send.at[(here.z + by) % NZ],
                z_recv.at[by - 1],
                z_sems,
                (by - 1,),
                here.step("z", by),
            )
        )
    for copy in pieces:
        copy.wait_recv()
    for t, out_ref in enumerate((key_ref, value_ref)):
        whole = final[here.z, t]
        for i in range(NZ - 1):
            whole = whole + z_recv[i, t].astype(F32)
        out_ref[...] = whole.T
    for copy in sent:
        copy.wait_send()


def weight_grads(x, g):
    vmem = pl.BlockSpec(memory_space=pltpu.VMEM)
    return pl.pallas_call(
        weight_kernel,
        out_shape=[jax.ShapeDtypeStruct((TILE, 32), F32)] * 2,
        in_specs=[vmem] * 2,
        out_specs=[vmem] * 2,
        scratch_shapes=[
            pltpu.VMEM((2, 2, 4, TILE, TILE), BF),
            pltpu.VMEM((2, 4, TILE, TILE), BF),
            pltpu.VMEM((2, 4, TILE, TILE), BF),
            pltpu.VMEM((2, 2, 2, TILE, TILE), BF),
            pltpu.VMEM((2, 2, 4, TILE, TILE), BF),
            pltpu.VMEM((2, 2, 4, TILE, TILE), BF),
            pltpu.VMEM((2, TILE, TILE), BF),
            pltpu.VMEM((2, 2, 128, TILE), BF),
            pltpu.VMEM((2, 2, TILE, TILE), BF),
            pltpu.VMEM((2, 2, TILE, TILE), BF),
            pltpu.VMEM((2, 3, TILE, TILE), F32),
            pltpu.VMEM((NZ, 2, 32, TILE), F32),
            pltpu.VMEM((NZ, 2, 32, TILE), BF),
            pltpu.VMEM((NZ - 1, 2, 32, TILE), BF),
            pltpu.SemaphoreType.DMA((2, RING + 2)),
            pltpu.SemaphoreType.DMA((2, 2, 12)),
            pltpu.SemaphoreType.DMA((2, NZ - 1)),
        ],
        compiler_params=pltpu.CompilerParams(
            collective_id=0, has_side_effects=True, vmem_limit_bytes=40 * 1024 * 1024
        ),
    )(x, g)


def solution(mesh):
    return jax.shard_map(
        shards,
        mesh=mesh,
        in_specs=(
            P("fsdp", "tm", None),
            P("fsdp", "tm", None),
            P("fsdp", "tm", None),
            P("fsdp", "tm", None),
            P("fsdp", "tm", None),
            P("fsdp", None),
            P("fsdp", None),
            P("tm", None, None),
            P("tm"),
        ),
        out_specs=(P("fsdp", "tm", None), P("fsdp", "tm", None), P("fsdp", "tm"), P("fsdp", "tm")),
        check_vma=False,
    )
```

```python
import jax
import jax.numpy as jnp
from jax import lax
from jax.experimental import pallas as pl
from jax.experimental.pallas import tpu as pltpu
from jax.sharding import PartitionSpec as P

H = 8
HS = 128
BLK = 128
TOK = 256
HD = 1024
D = 2048
MAXP = 8
BF = jnp.bfloat16
F32 = jnp.float32
MESH = pl.DeviceIdType.MESH
RING = 4
NZ = 8
NTM = RING * NZ
NF = 8
TILE = 256
KEYS = 640
HALO = 384
SCALE = HS**-0.5
NN = (((1,), (0,)), ((), ()))
NT = (((1,), (1,)), ((), ()))
TN = (((0,), (0,)), ((), ()))


def mm(a, b, dims):
    return lax.dot_general(a, b, dims, preferred_element_type=F32)


class Place:
    def __init__(self):
        self.tm = lax.axis_index("tm")
        self.fsdp = lax.axis_index("fsdp")
        self.z, self.y = self.tm // RING, self.tm % RING
        self.x, self.core = self.fsdp // 2, self.fsdp % 2

    def at(self, x=None, core=None, z=None, y=None):
        x = self.x if x is None else x
        core = self.core if core is None else core
        z = self.z if z is None else z
        y = self.y if y is None else y
        return (z * RING + y, x * 2 + core)

    def step(self, axis, by):
        if axis == "x":
            return self.at(x=(self.x + by) % RING)
        if axis == "y":
            return self.at(y=(self.y + by) % RING)
        return self.at(z=(self.z + by) % NZ)

    def partner(self):
        return self.at(core=1 - self.core)

    def later(self):
        return ((self.tm + 1) % NTM, self.fsdp)

    def earlier(self):
        return ((self.tm + NTM - 1) % NTM, self.fsdp)


def greet(devices):
    barrier = pltpu.get_barrier_semaphore()
    for device in devices:
        pl.semaphore_signal(barrier, inc=1, device_id=device, device_id_type=MESH)
    pl.semaphore_wait(barrier, len(devices))


def whole_kernel(
    x_ref,
    q_ref,
    k_ref,
    v_ref,
    do_ref,
    wk_ref,
    wv_ref,
    pairs_ref,
    count_ref,
    dq_ref,
    dx_ref,
    key_ref,
    value_ref,
    bias,
    kwin,
    vwin,
    own,
    far_send,
    far_recv,
    near_hold,
    near_send,
    near_recv,
    wbuf,
    g,
    gt,
    xs,
    opp_send,
    opp_recv,
    nb_send,
    nb_recv,
    opp2_send,
    opp2_recv,
    nb2_send,
    nb2_recv,
    sums,
    final,
    z_send,
    z_recv,
    halo_sems,
    relay_sems,
    far_sems,
    near_sems,
    w_sems,
    x_sems,
    gt_sems,
    ring_sems,
    z_sems,
    local_sems,
):
    here = Place()
    later, earlier, partner = here.later(), here.earlier(), here.partner()
    greet(
        [partner, later, earlier]
        + [here.step(axis, by) for axis in ("x", "y") for by in (1, 3)]
        + [here.step("z", by) for by in range(1, NZ)]
    )
    sent = []

    def remote(src, dst, sems, at, device):
        return pltpu.make_async_remote_copy(
            src_ref=src,
            dst_ref=dst,
            send_sem=sems.at[(0,) + at],
            recv_sem=sems.at[(1,) + at],
            device_id=device,
            device_id_type=MESH,
        )

    def send(src, dst, sems, at, device):
        copy = remote(src, dst, sems, at, device)
        copy.start()
        sent.append(copy)
        return copy

    def lanes(h):
        return pl.ds(pl.multiple_of(h * HS, HS), HS)

    def halo(h):
        return [
            remote(ref.at[:, lanes(h)], win.at[h, pl.ds(BLK, TOK)], halo_sems, (i, h), later)
            for i, (ref, win) in enumerate(((k_ref, kwin), (v_ref, vwin)))
        ]

    def relay(h):
        return [
            remote(win.at[h, pl.ds(2 * BLK, BLK)], win.at[h, pl.ds(0, BLK)], relay_sems, (i, h), later)
            for i, win in enumerate((kwin, vwin))
        ]

    def far(h):
        return remote(far_send.at[h], far_recv.at[h], far_sems, (h,), earlier)

    def near(h, block):
        return remote(near_send.at[h, block], near_recv.at[h, block], near_sems, (block, h), earlier)

    def turned(h):
        rows = pl.ds(pl.multiple_of(h * 32, 32), 32)
        return remote(gt.at[0, :, :, rows], gt.at[1, :, :, rows], gt_sems, (h,), partner)

    def start(copies):
        for copy in copies:
            copy.start()

    def arrive(copies):
        for copy in copies:
            copy.wait_recv()

    start(halo(0))
    start(halo(1))

    weights = (wk_ref, wv_ref)
    right, left = here.step("x", 1), here.step("x", 3)
    mine = here.fsdp
    left_id = ((here.x + 3) % RING) * 2 + here.core
    right_id = ((here.x + 1) % RING) * 2 + here.core
    opp_id = ((here.x + 2) % RING) * 2 + here.core
    from_left, from_right = {}, {}
    for i in (0, 1):
        from_left[i] = send(weights[i], wbuf.at[mine, i], w_sems, (i,), right)
        from_right[1 - i] = send(weights[1 - i], wbuf.at[mine, 1 - i], w_sems, (2 + 1 - i,), left)
    crossed = []
    for i in (0, 1):
        crossed.append(send(weights[i], wbuf.at[mine, i], w_sems, (6 + i,), partner))
    local = [
        pltpu.make_async_copy(weights[i], wbuf.at[mine, i], local_sems.at[i]) for i in (0, 1)
    ]
    for copy in local:
        copy.start()
    x_cross = []
    for xp in range(RING):
        theirs = pl.multiple_of(xp * 512 + (1 - here.core) * TILE, TILE)
        x_cross.append(send(x_ref.at[:, pl.ds(theirs, TILE)], xs.at[1, xp], x_sems, (xp,), partner))

    def forward_weights():
        from_left[0].wait_recv()
        opp_k = send(wbuf.at[left_id, 0], wbuf.at[left_id, 0], w_sems, (4,), right)
        crossed.append(send(wbuf.at[left_id, 0], wbuf.at[left_id, 0], w_sems, (8,), partner))
        from_right[1].wait_recv()
        opp_v = send(wbuf.at[right_id, 1], wbuf.at[right_id, 1], w_sems, (5,), left)
        crossed.append(send(wbuf.at[right_id, 1], wbuf.at[right_id, 1], w_sems, (9,), partner))
        return opp_k, opp_v

    def cross_weights(opp_k, opp_v):
        from_left[1].wait_recv()
        crossed.append(send(wbuf.at[left_id, 1], wbuf.at[left_id, 1], w_sems, (10,), partner))
        from_right[0].wait_recv()
        crossed.append(send(wbuf.at[right_id, 0], wbuf.at[right_id, 0], w_sems, (11,), partner))
        opp_k.wait_recv()
        crossed.append(send(wbuf.at[opp_id, 0], wbuf.at[opp_id, 0], w_sems, (12,), partner))
        opp_v.wait_recv()
        crossed.append(send(wbuf.at[opp_id, 1], wbuf.at[opp_id, 1], w_sems, (13,), partner))

    for xp in range(RING):
        own_columns = pl.multiple_of(xp * 512 + here.core * TILE, TILE)
        xs[0, xp] = x_ref[:, pl.ds(own_columns, TILE)]

    key_at = lax.broadcasted_iota(jnp.int32, (BLK, BLK), 0)
    query_at = lax.broadcasted_iota(jnp.int32, (BLK, BLK), 1)
    for qb in range(2):
        for kb in range(4):
            query_block = here.tm * 2 + qb
            key_block = query_block - 3 + kb
            hit = None
            for r in range(MAXP):
                same = (
                    (r < count_ref[0])
                    & (pairs_ref[r, 0] == query_block)
                    & (pairs_ref[r, 1] == key_block)
                )
                hit = same if hit is None else hit | same
            level = jnp.full((BLK, BLK), jnp.where(hit, 0.0, -jnp.inf), F32)
            if kb == 3:
                level = jnp.where(key_at <= query_at, level, -jnp.inf)
            bias[qb, kb * BLK : (kb + 1) * BLK] = level

    def head(h):
        query, cotangent = q_ref[:, lanes(h)], do_ref[:, lanes(h)]
        keys = jnp.concatenate([kwin[h], k_ref[:, lanes(h)]], axis=0)
        values = jnp.concatenate([vwin[h], v_ref[:, lanes(h)]], axis=0)
        scores = mm(keys, query, NT)
        grad_probs = mm(values, cotangent, NT)
        probs_parts, grads_parts = [], []
        for qb in range(2):
            rows, columns = slice(qb * BLK, qb * BLK + 512), slice(qb * BLK, qb * BLK + BLK)
            score = scores[rows, columns] * SCALE + bias[qb]
            prob = jnp.exp(score - jnp.max(score, axis=0, keepdims=True))
            prob = prob * (1.0 / jnp.sum(prob, axis=0, keepdims=True))
            low = prob.astype(BF)
            grad = grad_probs[rows, columns]
            row_dot = jnp.sum(low.astype(F32) * grad, axis=0, keepdims=True)
            probs_parts.append(low)
            grads_parts.append((prob * (grad - row_dot)).astype(BF))

        def laid(parts):
            blank = jnp.zeros((BLK, BLK), BF)
            return jnp.concatenate(
                [
                    jnp.concatenate([parts[0], blank], axis=0),
                    jnp.concatenate([blank, parts[1]], axis=0),
                ],
                axis=1,
            )

        probs_low, grads_low = laid(probs_parts), laid(grads_parts)
        dq_ref[:, lanes(h)] = (mm(grads_low, keys, TN) * SCALE).astype(BF)
        for i, full in enumerate((mm(grads_low, query, NN) * SCALE, mm(probs_low, cotangent, NN))):
            far_send[h, i] = full[:BLK].astype(BF)
            near_send[h, 0, i] = full[BLK : 2 * BLK].astype(BF)
            near_hold[h % 2, i] = full[2 * BLK : 3 * BLK]
            own[h, i] = full[3 * BLK :]
        far(h).start()
        near(h, 0).start()

    def pass_on(h):
        far(h).wait_recv()
        for i in range(2):
            near_send[h, 1, i] = (near_hold[h % 2, i] + far_recv[h, i].astype(F32)).astype(BF)
        near(h, 1).start()

    def settle(h):
        arrive([near(h, 0), near(h, 1)])
        for i in range(2):
            blocks = [
                own[h, i, b * BLK : (b + 1) * BLK] + near_recv[h, b, i].astype(F32) for b in range(2)
            ]
            low = jnp.concatenate(blocks, axis=0).astype(BF)
            g[i, :, lanes(h)] = low
            flipped = low.T
            rows = pl.ds(pl.multiple_of(h * 32, 32), 32)
            for yp in range(RING):
                gt[0, i, yp, rows] = flipped[yp * 32 : yp * 32 + 32]
        turned(h).start()

    arrive(halo(0))
    start(relay(0))

    def body(h, carry, first=False, second=False, more=True, last=False):
        if more:
            start(halo(h + 2))
        if not last:
            arrive(halo(h + 1))
            start(relay(h + 1))
        arrive(relay(h))
        head(h)
        if not first:
            pass_on(h - 1)
            if not second:
                settle(h - 2)
        return carry

    body(0, 0, first=True)
    body(1, 0, second=True)
    lax.fori_loop(2, 4, body, 0)
    opp = forward_weights()
    lax.fori_loop(4, 6, body, 0)
    body(6, 0, more=False)
    body(7, 0, more=False, last=True)
    pass_on(7)
    settle(6)
    settle(7)
    cross_weights(*opp)
    for copy in x_cross:
        copy.wait_recv()
    arrive([turned(h) for h in range(H)])

    axes = (("x", "y"), ("y", "x"))
    place = {"x": here.x, "y": here.y}

    def block(t, ring, b):
        xp, yp = (ring, b) if t == 0 else (b, ring)
        return mm(gt[0, t, yp], xs[0, xp], NN) + mm(gt[1, t, yp], xs[1, xp], NN)

    def input_rows(f, carry):
        columns = pl.ds(pl.multiple_of(f * TILE, TILE), TILE)
        dx_ref[:, columns] = (mm(g[0], wbuf[f, 0], NT) + mm(g[1], wbuf[f, 1], NT)).astype(BF)
        return carry

    first, pieces = [], []
    for t in range(2):
        axis = axes[t][0]
        opp = (place[axis] + 2) % RING
        for b in range(4):
            opp_send[t, b] = block(t, opp, b).astype(BF)
        first.append(
            [
                send(
                    opp_send.at[t, pl.ds(2 * d, 2)],
                    opp_recv.at[t, d],
                    ring_sems,
                    (t, d),
                    here.step(axis, (1, 3)[d]),
                )
                for d in range(2)
            ]
        )
    for t in range(2):
        axis = axes[t][0]
        for d in range(2):
            ring = (place[axis] + (1, 3)[d]) % RING
            lo = (2, 0)[d]
            for b in (lo, lo + 1):
                nb_send[t, d, b] = block(t, ring, b).astype(BF)
            pieces.append(
                send(
                    nb_send.at[t, d, pl.ds(lo, 2)],
                    nb_recv.at[t, d, pl.ds(lo, 2)],
                    ring_sems,
                    (t, 2 + d),
                    here.step(axis, (1, 3)[d]),
                )
            )
    for copy in crossed:
        copy.wait_recv()
    for copy in local:
        copy.wait()
    lax.fori_loop(0, 4, input_rows, 0)
    for t in range(2):
        axis = axes[t][0]
        for d in range(2):
            ring = (place[axis] + (1, 3)[d]) % RING
            lo = (0, 2)[d]
            first[t][d].wait_recv()
            for b in (lo, lo + 1):
                nb_send[t, d, b] = (
                    block(t, ring, b) + opp_recv[t, d, b - lo].astype(F32)
                ).astype(BF)
            pieces.append(
                send(
                    nb_send.at[t, d, pl.ds(lo, 2)],
                    nb_recv.at[t, d, pl.ds(lo, 2)],
                    ring_sems,
                    (t, 4 + d),
                    here.step(axis, (1, 3)[d]),
                )
            )
    lax.fori_loop(4, 8, input_rows, 0)
    for copy in pieces:
        copy.wait_recv()

    second = []
    for t in range(2):
        axis1, axis2 = axes[t]

        def total(b):
            return (
                block(t, place[axis1], b)
                + nb_recv[t, 0, b].astype(F32)
                + nb_recv[t, 1, b].astype(F32)
            )

        opp2_send[t] = total((place[axis2] + 2) % RING).astype(BF)
        second.append(
            [
                send(
                    opp2_send.at[t, pl.ds(128 * d, 128)],
                    opp2_recv.at[t, d],
                    ring_sems,
                    (t, 6 + d),
                    here.step(axis2, (1, 3)[d]),
                )
                for d in range(2)
            ]
        )
        for d in range(2):
            sums[t, d] = total((place[axis2] + (1, 3)[d]) % RING)
        sums[t, 2] = total(place[axis2])
    pieces = []
    for t in range(2):
        for d in range(2):
            lo = (128, 0)[d]
            nb2_send[t, d, lo : lo + 128] = sums[t, d, lo : lo + 128].astype(BF)
            pieces.append(
                send(
                    nb2_send.at[t, d, pl.ds(lo, 128)],
                    nb2_recv.at[t, d, pl.ds(lo, 128)],
                    ring_sems,
                    (t, 8 + d),
                    here.step(axes[t][1], (1, 3)[d]),
                )
            )
    for t in range(2):
        for d in range(2):
            lo = (0, 128)[d]
            second[t][d].wait_recv()
            nb2_send[t, d, lo : lo + 128] = (
                sums[t, d, lo : lo + 128] + opp2_recv[t, d].astype(F32)
            ).astype(BF)
            pieces.append(
                send(
                    nb2_send.at[t, d, pl.ds(lo, 128)],
                    nb2_recv.at[t, d, pl.ds(lo, 128)],
                    ring_sems,
                    (t, 10 + d),
                    here.step(axes[t][1], (1, 3)[d]),
                )
            )
    for copy in pieces:
        copy.wait_recv()
    for t in range(2):
        whole = sums[t, 2] + nb2_recv[t, 0].astype(F32) + nb2_recv[t, 1].astype(F32)
        for zp in range(NZ):
            part = whole[zp * 32 : zp * 32 + 32]
            final[zp, t] = part
            z_send[zp, t] = part.astype(BF)
    pieces = []
    for by in range(1, NZ):
        pieces.append(
            send(
                z_send.at[(here.z + by) % NZ],
                z_recv.at[by - 1],
                z_sems,
                (by - 1,),
                here.step("z", by),
            )
        )
    for copy in pieces:
        copy.wait_recv()
    for t, out_ref in enumerate((key_ref, value_ref)):
        whole = final[here.z, t]
        for i in range(NZ - 1):
            whole = whole + z_recv[i, t].astype(F32)
        out_ref[...] = whole.T
    for copy in sent:
        copy.wait_send()

    def drain(h, carry):
        for copy in halo(h) + relay(h) + [far(h), near(h, 0), near(h, 1), turned(h)]:
            copy.wait_send()
        return carry

    lax.fori_loop(0, H, drain, 0)


def shards(
    inputs,
    query_rows,
    saved_key_rows,
    value_rows,
    grad_out,
    key_weight,
    value_weight,
    block_pairs,
    pair_counts,
):
    vmem = pl.BlockSpec(memory_space=pltpu.VMEM)
    smem = pl.BlockSpec(memory_space=pltpu.SMEM)
    grad_query, input_gradient, key_total, value_total = pl.pallas_call(
        whole_kernel,
        out_shape=[
            jax.ShapeDtypeStruct((TOK, HD), BF),
            jax.ShapeDtypeStruct((TOK, D), BF),
            jax.ShapeDtypeStruct((TILE, 32), F32),
            jax.ShapeDtypeStruct((TILE, 32), F32),
        ],
        in_specs=[vmem] * 7 + [smem] * 2,
        out_specs=[vmem] * 4,
        scratch_shapes=[
            pltpu.VMEM((2, 512, BLK), F32),
            pltpu.VMEM((H, HALO, HS), BF),
            pltpu.VMEM((H, HALO, HS), BF),
            pltpu.VMEM((H, 2, TOK, HS), F32),
            pltpu.VMEM((H, 2, BLK, HS), BF),
            pltpu.VMEM((H, 2, BLK, HS), BF),
            pltpu.VMEM((2, 2, BLK, HS), F32),
            pltpu.VMEM((H, 2, 2, BLK, HS), BF),
            pltpu.VMEM((H, 2, 2, BLK, HS), BF),
            pltpu.VMEM((NF, 2, TILE, HD), BF),
            pltpu.VMEM((2, TOK, HD), BF),
            pltpu.VMEM((2, 2, 4, TILE, TILE), BF),
            pltpu.VMEM((2, 4, TILE, TILE), BF),
            pltpu.VMEM((2, 4, TILE, TILE), BF),
            pltpu.VMEM((2, 2, 2, TILE, TILE), BF),
            pltpu.VMEM((2, 2, 4, TILE, TILE), BF),
            pltpu.VMEM((2, 2, 4, TILE, TILE), BF),
            pltpu.VMEM((2, TILE, TILE), BF),
            pltpu.VMEM((2, 2, 128, TILE), BF),
            pltpu.VMEM((2, 2, TILE, TILE), BF),
            pltpu.VMEM((2, 2, TILE, TILE), BF),
            pltpu.VMEM((2, 3, TILE, TILE), F32),
            pltpu.VMEM((NZ, 2, 32, TILE), F32),
            pltpu.VMEM((NZ, 2, 32, TILE), BF),
            pltpu.VMEM((NZ - 1, 2, 32, TILE), BF),
            pltpu.SemaphoreType.DMA((2, 2, H)),
            pltpu.SemaphoreType.DMA((2, 2, H)),
            pltpu.SemaphoreType.DMA((2, H)),
            pltpu.SemaphoreType.DMA((2, 2, H)),
            pltpu.SemaphoreType.DMA((2, 14)),
            pltpu.SemaphoreType.DMA((2, RING)),
            pltpu.SemaphoreType.DMA((2, H)),
            pltpu.SemaphoreType.DMA((2, 2, 12)),
            pltpu.SemaphoreType.DMA((2, NZ - 1)),
            pltpu.SemaphoreType.DMA((2,)),
        ],
        compiler_params=pltpu.CompilerParams(
            collective_id=0, has_side_effects=True, vmem_limit_bytes=56 * 1024 * 1024
        ),
    )(
        inputs[0],
        query_rows[0],
        saved_key_rows[0],
        value_rows[0],
        grad_out[0],
        key_weight,
        value_weight,
        block_pairs[0],
        pair_counts,
    )
    return (grad_query[None], input_gradient[None], key_total, value_total)


def solution(mesh):
    return jax.shard_map(
        shards,
        mesh=mesh,
        in_specs=(
            P("fsdp", "tm", None),
            P("fsdp", "tm", None),
            P("fsdp", "tm", None),
            P("fsdp", "tm", None),
            P("fsdp", "tm", None),
            P("fsdp", None),
            P("fsdp", None),
            P("tm", None, None),
            P("tm"),
        ),
        out_specs=(P("fsdp", "tm", None), P("fsdp", "tm", None), P("fsdp", "tm"), P("fsdp", "tm")),
        check_vma=False,
    )
```

```python
import jax
import jax.numpy as jnp
from jax import lax
from jax.experimental import pallas as pl
from jax.experimental.pallas import tpu as pltpu
from jax.sharding import PartitionSpec as P

H = 8
HS = 128
BLK = 128
TOK = 256
HD = 1024
D = 2048
MAXP = 8
BF = jnp.bfloat16
F32 = jnp.float32
MESH = pl.DeviceIdType.MESH
RING = 4
NZ = 8
NTM = RING * NZ
NF = 8
TILE = 256
KEYS = 640
HALO = 384
SCALE = HS**-0.5
NN = (((1,), (0,)), ((), ()))
NT = (((1,), (1,)), ((), ()))
TN = (((0,), (0,)), ((), ()))


def mm(a, b, dims):
    return lax.dot_general(a, b, dims, preferred_element_type=F32)


class Place:
    def __init__(self):
        self.tm = lax.axis_index("tm")
        self.fsdp = lax.axis_index("fsdp")
        self.z, self.y = self.tm // RING, self.tm % RING
        self.x, self.core = self.fsdp // 2, self.fsdp % 2

    def at(self, x=None, core=None, z=None, y=None):
        x = self.x if x is None else x
        core = self.core if core is None else core
        z = self.z if z is None else z
        y = self.y if y is None else y
        return (z * RING + y, x * 2 + core)

    def step(self, axis, by):
        if axis == "x":
            return self.at(x=(self.x + by) % RING)
        if axis == "y":
            return self.at(y=(self.y + by) % RING)
        return self.at(z=(self.z + by) % NZ)

    def partner(self):
        return self.at(core=1 - self.core)

    def later(self, by):
        return ((self.tm + NTM + by) % NTM, self.fsdp)


def greet(devices):
    barrier = pltpu.get_barrier_semaphore()
    for device in devices:
        pl.semaphore_signal(barrier, inc=1, device_id=device, device_id_type=MESH)
    pl.semaphore_wait(barrier, len(devices))


def whole_kernel(
    x_hbm,
    q_hbm,
    k_hbm,
    v_hbm,
    do_hbm,
    wk_hbm,
    wv_hbm,
    pairs_ref,
    count_ref,
    dq_hbm,
    dx_hbm,
    key_ref,
    value_ref,
    q_ref,
    k_ref,
    v_ref,
    do_ref,
    dq,
    dx,
    bias,
    kwin,
    vwin,
    qwin,
    cwin,
    own,
    stat_send,
    stat_near,
    stat_far,
    wbuf,
    g,
    gt,
    xs,
    opp_send,
    opp_recv,
    nb_send,
    nb_recv,
    opp2_send,
    opp2_recv,
    nb2_send,
    nb2_recv,
    sums,
    final,
    z_send,
    z_recv,
    halo_sems,
    relay_sems,
    stat_sems,
    w_sems,
    x_sems,
    gt_sems,
    ring_sems,
    ring2_sems,
    z_sems,
    local_sems,
):
    here = Place()
    later, earlier, partner = here.later(1), here.later(-1), here.partner()
    earlier2 = here.later(-2)

    loads = [
        pltpu.make_async_copy(src, dst, local_sems.at[i])
        for i, (src, dst) in enumerate(
            ((k_hbm, k_ref), (q_hbm, q_ref), (v_hbm, v_ref), (do_hbm, do_ref))
        )
    ]
    own_rows = []
    for i, src in enumerate((wk_hbm, wv_hbm)):
        own_rows.append(pltpu.make_async_copy(src, wbuf.at[here.fsdp, i], local_sems.at[4 + i]))
    for xp in range(RING):
        columns = pl.ds(pl.multiple_of(xp * 512 + here.core * TILE, TILE), TILE)
        own_rows.append(pltpu.make_async_copy(x_hbm.at[:, columns], xs.at[0, xp], local_sems.at[6 + xp]))
    for copy in loads + own_rows:
        copy.start()

    greet(
        [partner, later, earlier, here.later(2), earlier2]
        + [here.step(axis, by) for axis in ("x", "y") for by in (1, 3)]
        + [here.step("z", by) for by in range(1, NZ)]
    )
    sent = []

    def remote(src, dst, sems, at, device):
        return pltpu.make_async_remote_copy(
            src_ref=src,
            dst_ref=dst,
            send_sem=sems.at[(0,) + at],
            recv_sem=sems.at[(1,) + at],
            device_id=device,
            device_id_type=MESH,
        )

    def send(src, dst, sems, at, device):
        copy = remote(src, dst, sems, at, device)
        copy.start()
        sent.append(copy)
        return copy

    def lanes(h):
        return pl.ds(pl.multiple_of(h * HS, HS), HS)

    streams = (
        (k_hbm, kwin, BLK, 2 * BLK, 0, later),
        (v_hbm, vwin, BLK, 2 * BLK, 0, later),
        (q_hbm, qwin, 0, 0, 2 * BLK, earlier),
        (do_hbm, cwin, 0, 0, 2 * BLK, earlier),
    )

    def halo(h):
        return [
            remote(ref.at[:, lanes(h)], win.at[h, pl.ds(at, TOK)], halo_sems, (i, h), device)
            for i, (ref, win, at, _, _, device) in enumerate(streams)
        ]

    def relay(h, which=range(4)):
        copies = []
        for i in which:
            _, win, _, src, dst, device = streams[i]
            copies.append(
                remote(win.at[h, pl.ds(src, BLK)], win.at[h, pl.ds(dst, BLK)], relay_sems, (i, h), device)
            )
        return copies

    def stats(h):
        return [
            remote(stat_send.at[h], stat_near.at[h], stat_sems, (0, h), earlier),
            remote(stat_send.at[h, :, pl.ds(0, BLK)], stat_far.at[h], stat_sems, (1, h), earlier2),
        ]

    def turned(h):
        rows = pl.ds(pl.multiple_of(h * 32, 32), 32)
        return remote(gt.at[0, :, :, rows], gt.at[1, :, :, rows], gt_sems, (h,), partner)

    def start(copies):
        for copy in copies:
            copy.start()

    def arrive(copies):
        for copy in copies:
            copy.wait_recv()

    start(halo(0))
    start(halo(1))

    weights = (wk_hbm, wv_hbm)
    right, left = here.step("x", 1), here.step("x", 3)
    mine = here.fsdp
    left_id = ((here.x + 3) % RING) * 2 + here.core
    right_id = ((here.x + 1) % RING) * 2 + here.core
    opp_id = ((here.x + 2) % RING) * 2 + here.core
    from_left, from_right = {}, {}
    for i in (0, 1):
        from_left[i] = send(weights[i], wbuf.at[mine, i], w_sems, (i,), right)
        from_right[1 - i] = send(weights[1 - i], wbuf.at[mine, 1 - i], w_sems, (2 + 1 - i,), left)
    crossed = []
    for i in (0, 1):
        crossed.append(send(weights[i], wbuf.at[mine, i], w_sems, (6 + i,), partner))
    x_cross = []
    for xp in range(RING):
        theirs = pl.multiple_of(xp * 512 + (1 - here.core) * TILE, TILE)
        x_cross.append(send(x_hbm.at[:, pl.ds(theirs, TILE)], xs.at[1, xp], x_sems, (xp,), partner))

    def forward_weights():
        from_left[0].wait_recv()
        opp_k = send(wbuf.at[left_id, 0], wbuf.at[left_id, 0], w_sems, (4,), right)
        crossed.append(send(wbuf.at[left_id, 0], wbuf.at[left_id, 0], w_sems, (8,), partner))
        from_right[1].wait_recv()
        opp_v = send(wbuf.at[right_id, 1], wbuf.at[right_id, 1], w_sems, (5,), left)
        crossed.append(send(wbuf.at[right_id, 1], wbuf.at[right_id, 1], w_sems, (9,), partner))
        return opp_k, opp_v

    def cross_weights(opp_k, opp_v):
        from_left[1].wait_recv()
        crossed.append(send(wbuf.at[left_id, 1], wbuf.at[left_id, 1], w_sems, (10,), partner))
        from_right[0].wait_recv()
        crossed.append(send(wbuf.at[right_id, 0], wbuf.at[right_id, 0], w_sems, (11,), partner))
        opp_k.wait_recv()
        crossed.append(send(wbuf.at[opp_id, 0], wbuf.at[opp_id, 0], w_sems, (12,), partner))
        opp_v.wait_recv()
        crossed.append(send(wbuf.at[opp_id, 1], wbuf.at[opp_id, 1], w_sems, (13,), partner))

    key_at = lax.broadcasted_iota(jnp.int32, (BLK, BLK), 0)
    query_at = lax.broadcasted_iota(jnp.int32, (BLK, BLK), 1)
    levels = {}
    for qb in range(2):
        for kb in range(4):
            query_block = here.tm * 2 + qb
            key_block = query_block - 3 + kb
            hit = None
            for r in range(MAXP):
                same = (
                    (r < count_ref[0])
                    & (pairs_ref[0, r] == query_block)
                    & (pairs_ref[1, r] == key_block)
                )
                hit = same if hit is None else hit | same
            levels[qb, kb] = jnp.where(hit, 0.0, -jnp.inf)
            level = jnp.full((BLK, BLK), levels[qb, kb], F32)
            if kb == 3:
                level = jnp.where(key_at <= query_at, level, -jnp.inf)
            bias[qb, kb * BLK : (kb + 1) * BLK] = level
    rows = [
        jnp.concatenate([jnp.full((1, BLK), levels[0, a], F32), jnp.full((1, BLK), levels[1, b], F32)], axis=1)
        for a, b in ((1, 0), (2, 1), (0, 0))
    ]
    for h in range(H):
        for i, row in enumerate(rows):
            stat_send[h, 3 + i : 4 + i] = row

    def query_side(h):
        query, cotangent = q_ref[:, lanes(h)], do_ref[:, lanes(h)]
        keys = jnp.concatenate([kwin[h], k_ref[:, lanes(h)]], axis=0)
        values = jnp.concatenate([vwin[h], v_ref[:, lanes(h)]], axis=0)
        scores = mm(keys, query, NT)
        grad_probs = mm(values, cotangent, NT)
        probs_parts, grads_parts, noted = [], [], []
        for qb in range(2):
            near, columns = slice(qb * BLK, qb * BLK + 512), slice(qb * BLK, qb * BLK + BLK)
            score = scores[near, columns] * SCALE + bias[qb]
            most = jnp.max(score, axis=0, keepdims=True)
            prob = jnp.exp(score - most)
            share = 1.0 / jnp.sum(prob, axis=0, keepdims=True)
            prob = prob * share
            low = prob.astype(BF)
            grad = grad_probs[near, columns]
            row_dot = jnp.sum(low.astype(F32) * grad, axis=0, keepdims=True)
            probs_parts.append(low)
            grads_parts.append((prob * (grad - row_dot)).astype(BF))
            noted.append((most, share, row_dot))
        for i in range(3):
            stat_send[h, i : i + 1] = jnp.concatenate([noted[0][i], noted[1][i]], axis=1)
        start(stats(h))
        blank = jnp.zeros((BLK, BLK), BF)
        grads_low = jnp.concatenate(
            [
                jnp.concatenate([grads_parts[0], blank], axis=0),
                jnp.concatenate([blank, grads_parts[1]], axis=0),
            ],
            axis=1,
        )
        probs_own = jnp.concatenate(
            [jnp.concatenate([probs_parts[0][HALO:], blank], axis=0), probs_parts[1][2 * BLK :]],
            axis=1,
        )
        dq[:, lanes(h)] = (mm(grads_low, keys, TN) * SCALE).astype(BF)
        own[h % 2, 0] = mm(grads_low[HALO:], query, NN)
        own[h % 2, 1] = mm(probs_own, cotangent, NN)

    def key_side(h):
        arrive(relay(h, (2, 3)) + stats(h))
        query, cotangent = qwin[h], cwin[h]
        keys, values = k_ref[:, lanes(h)], v_ref[:, lanes(h)]
        scores = mm(keys, query, NT)
        grad_probs = mm(values, cotangent, NT)
        most, share, row_dot = (
            jnp.concatenate([stat_near[h, i : i + 1], stat_far[h, i : i + 1]], axis=1) for i in range(3)
        )
        never = jnp.full((1, BLK), -jnp.inf, F32)
        levels = (
            jnp.concatenate([stat_near[h, 3:4], never], axis=1),
            jnp.concatenate([stat_near[h, 4:5], stat_far[h, 5:6]], axis=1),
        )
        probs_parts, grads_parts = [], []
        for b in range(2):
            block = slice(b * BLK, b * BLK + BLK)
            prob = jnp.exp(scores[block] * SCALE + levels[b] - most) * share
            probs_parts.append(prob.astype(BF))
            grads_parts.append((prob * (grad_probs[block] - row_dot)).astype(BF))
        keys_grad = mm(jnp.concatenate(grads_parts, axis=0), query, NN)
        values_grad = mm(jnp.concatenate(probs_parts, axis=0), cotangent, NN)
        for i, full in enumerate(((own[h % 2, 0] + keys_grad) * SCALE, own[h % 2, 1] + values_grad)):
            low = full.astype(BF)
            g[i, :, lanes(h)] = low
            flipped = low.T
            rows = pl.ds(pl.multiple_of(h * 32, 32), 32)
            for yp in range(RING):
                gt[0, i, yp, rows] = flipped[yp * 32 : yp * 32 + 32]
        turned(h).start()

    for copy in loads:
        copy.wait()
    arrive(halo(0))
    start(relay(0))

    def body(h, carry, first=False, more=True, last=False):
        if more:
            start(halo(h + 2))
        if not last:
            arrive(halo(h + 1))
            start(relay(h + 1))
        arrive(relay(h, (0, 1)))
        query_side(h)
        if not first:
            key_side(h - 1)
        return carry

    body(0, 0, first=True)
    lax.fori_loop(1, 4, body, 0)
    opp_weights = forward_weights()
    lax.fori_loop(4, 6, body, 0)
    body(6, 0, more=False)
    body(7, 0, more=False, last=True)
    key_side(7)
    dq_out = pltpu.make_async_copy(dq, dq_hbm, local_sems.at[10])
    dq_out.start()
    for copy in own_rows:
        copy.wait()
    for copy in x_cross:
        copy.wait_recv()
    arrive([turned(h) for h in range(H)])

    axes = (("x", "y"), ("y", "x"))
    place = {"x": here.x, "y": here.y}
    slots = (2, 1, 3, 0)
    ways = (1, 3)

    def block(t, ring, slot):
        b = (place[axes[t][1]] + slots[slot]) % RING
        xp, yp = (ring, b) if t == 0 else (b, ring)
        return mm(gt[0, t, yp], xs[0, xp], NN) + mm(gt[1, t, yp], xs[1, xp], NN)

    def input_rows(f, carry):
        columns = pl.ds(pl.multiple_of(f * TILE, TILE), TILE)
        dx[:, columns] = (mm(g[0], wbuf[f, 0], NT) + mm(g[1], wbuf[f, 1], NT)).astype(BF)
        return carry

    def ring(t, d):
        return (place[axes[t][0]] + ways[d]) % RING

    opposite, beside = {}, {}
    for i in range(2):
        for t in range(2):
            opp = (place[axes[t][0]] + 2) % RING
            for d in range(2):
                slot = 2 * d + i
                opp_send[t, slot] = block(t, opp, slot).astype(BF)
                opposite[t, slot] = send(
                    opp_send.at[t, slot],
                    opp_recv.at[t, slot],
                    ring_sems,
                    (t, slot),
                    here.step(axes[t][0], ways[d]),
                )

    def give(t, d, slot, value):
        nb_send[t, d, slot] = value.astype(BF)
        beside[t, d, slot] = send(
            nb_send.at[t, d, slot],
            nb_recv.at[t, d, slot],
            ring_sems,
            (t, 4 + d * 4 + slot),
            here.step(axes[t][0], ways[d]),
        )

    for i in range(2):
        for t in range(2):
            for d in range(2):
                slot = 2 * (1 - d) + i
                give(t, d, slot, block(t, ring(t, d), slot))
    for i in range(2):
        for t in range(2):
            for d in range(2):
                slot = 2 * d + i
                opposite[t, slot].wait_recv()
                give(t, d, slot, block(t, ring(t, d), slot) + opp_recv[t, slot].astype(F32))
    cross_weights(*opp_weights)
    for copy in crossed:
        copy.wait_recv()
    lax.fori_loop(0, NF, input_rows, 0)
    dx_out = pltpu.make_async_copy(dx, dx_hbm, local_sems.at[11])
    dx_out.start()

    def total(t, slot):
        for d in range(2):
            beside[t, d, slot].wait_recv()
        return (
            block(t, place[axes[t][0]], slot)
            + nb_recv[t, 0, slot].astype(F32)
            + nb_recv[t, 1, slot].astype(F32)
        )

    second, pieces = {}, {}

    def give2(t, d, half, value):
        part = pl.ds(128 * half, 128)
        nb2_send[t, d, part] = value.astype(BF)
        pieces[t, d, half] = send(
            nb2_send.at[t, d, part],
            nb2_recv.at[t, d, part],
            ring2_sems,
            (t, 2 + 2 * d + half),
            here.step(axes[t][1], ways[d]),
        )

    for t in range(2):
        opp2_send[t] = total(t, 0).astype(BF)
        for d in range(2):
            second[t, d] = send(
                opp2_send.at[t, pl.ds(128 * d, 128)],
                opp2_recv.at[t, d],
                ring2_sems,
                (t, d),
                here.step(axes[t][1], ways[d]),
            )
    for d in range(2):
        for t in range(2):
            sums[t, d] = total(t, 1 + d)
            give2(t, d, 1 - d, sums[t, d, pl.ds(128 * (1 - d), 128)])
    for t in range(2):
        sums[t, 2] = total(t, 3)
    for t in range(2):
        for d in range(2):
            second[t, d].wait_recv()
            give2(t, d, d, sums[t, d, pl.ds(128 * d, 128)] + opp2_recv[t, d].astype(F32))
    spread = []
    for t in range(2):
        for d in range(2):
            for half in range(2):
                pieces[t, d, half].wait_recv()
        whole = sums[t, 2] + nb2_recv[t, 0].astype(F32) + nb2_recv[t, 1].astype(F32)
        for zp in range(NZ):
            part = whole[zp * 32 : zp * 32 + 32]
            final[t, zp] = part
            z_send[t, zp] = part.astype(BF)
        for by in range(1, NZ):
            spread.append(
                send(
                    z_send.at[t, (here.z + by) % NZ],
                    z_recv.at[t, by - 1],
                    z_sems,
                    (t, by - 1),
                    here.step("z", by),
                )
            )
    arrive(spread)
    for t, out_ref in enumerate((key_ref, value_ref)):
        whole = final[t, here.z]
        for i in range(NZ - 1):
            whole = whole + z_recv[t, i].astype(F32)
        out_ref[...] = whole
    dq_out.wait()
    dx_out.wait()
    for copy in sent:
        copy.wait_send()

    def drain(h, carry):
        for copy in halo(h) + relay(h) + stats(h) + [turned(h)]:
            copy.wait_send()
        return carry

    lax.fori_loop(0, H, drain, 0)


def hand_over(*refs):
    count = (len(refs) - 1) // 2
    copies = [
        pltpu.make_async_copy(refs[i], refs[count + i], refs[-1].at[i]) for i in range(count)
    ]
    for copy in copies:
        copy.start()
    for copy in copies:
        copy.wait()


def shards(
    inputs,
    query_rows,
    saved_key_rows,
    value_rows,
    grad_out,
    key_weight,
    value_weight,
    block_pairs,
    pair_counts,
):
    vmem = pl.BlockSpec(memory_space=pltpu.VMEM)
    smem = pl.BlockSpec(memory_space=pltpu.SMEM)
    anywhere = pl.BlockSpec(memory_space=pl.ANY)
    shapes = [
        jax.ShapeDtypeStruct((TOK, HD), BF),
        jax.ShapeDtypeStruct((TOK, D), BF),
        jax.ShapeDtypeStruct((32, TILE), F32),
        jax.ShapeDtypeStruct((32, TILE), F32),
    ]
    made = pl.pallas_call(
        whole_kernel,
        out_shape=shapes,
        in_specs=[anywhere] * 7 + [smem] * 2,
        out_specs=[anywhere] * 2 + [vmem] * 2,
        scratch_shapes=[
            pltpu.VMEM((TOK, HD), BF),
            pltpu.VMEM((TOK, HD), BF),
            pltpu.VMEM((TOK, HD), BF),
            pltpu.VMEM((TOK, HD), BF),
            pltpu.VMEM((TOK, HD), BF),
            pltpu.VMEM((TOK, D), BF),
            pltpu.VMEM((2, 512, BLK), F32),
            pltpu.VMEM((H, HALO, HS), BF),
            pltpu.VMEM((H, HALO, HS), BF),
            pltpu.VMEM((H, HALO, HS), BF),
            pltpu.VMEM((H, HALO, HS), BF),
            pltpu.VMEM((2, 2, TOK, HS), F32),
            pltpu.VMEM((H, 8, TOK), F32),
            pltpu.VMEM((H, 8, TOK), F32),
            pltpu.VMEM((H, 8, BLK), F32),
            pltpu.VMEM((NF, 2, TILE, HD), BF),
            pltpu.VMEM((2, TOK, HD), BF),
            pltpu.VMEM((2, 2, 4, TILE, TILE), BF),
            pltpu.VMEM((2, 4, TILE, TILE), BF),
            pltpu.VMEM((2, 4, TILE, TILE), BF),
            pltpu.VMEM((2, 4, TILE, TILE), BF),
            pltpu.VMEM((2, 2, 4, TILE, TILE), BF),
            pltpu.VMEM((2, 2, 4, TILE, TILE), BF),
            pltpu.VMEM((2, TILE, TILE), BF),
            pltpu.VMEM((2, 2, 128, TILE), BF),
            pltpu.VMEM((2, 2, TILE, TILE), BF),
            pltpu.VMEM((2, 2, TILE, TILE), BF),
            pltpu.VMEM((2, 3, TILE, TILE), F32),
            pltpu.VMEM((2, NZ, 32, TILE), F32),
            pltpu.VMEM((2, NZ, 32, TILE), BF),
            pltpu.VMEM((2, NZ - 1, 32, TILE), BF),
            pltpu.SemaphoreType.DMA((2, 4, H)),
            pltpu.SemaphoreType.DMA((2, 4, H)),
            pltpu.SemaphoreType.DMA((2, 2, H)),
            pltpu.SemaphoreType.DMA((2, 14)),
            pltpu.SemaphoreType.DMA((2, RING)),
            pltpu.SemaphoreType.DMA((2, H)),
            pltpu.SemaphoreType.DMA((2, 2, 12)),
            pltpu.SemaphoreType.DMA((2, 2, 6)),
            pltpu.SemaphoreType.DMA((2, 2, NZ - 1)),
            pltpu.SemaphoreType.DMA((12,)),
        ],
        compiler_params=pltpu.CompilerParams(
            collective_id=0, has_side_effects=True, vmem_limit_bytes=56 * 1024 * 1024
        ),
    )(
        inputs[0],
        query_rows[0],
        saved_key_rows[0],
        value_rows[0],
        grad_out[0],
        key_weight,
        value_weight,
        block_pairs[0].T,
        pair_counts,
    )
    grad_query, input_gradient, key_total, value_total = pl.pallas_call(
        hand_over,
        out_shape=shapes,
        in_specs=[vmem] * 4,
        out_specs=[anywhere] * 4,
        scratch_shapes=[pltpu.SemaphoreType.DMA((4,))],
    )(*made)
    return (grad_query[None], input_gradient[None], key_total.T, value_total.T)


def solution(mesh):
    return jax.shard_map(
        shards,
        mesh=mesh,
        in_specs=(
            P("fsdp", "tm", None),
            P("fsdp", "tm", None),
            P("fsdp", "tm", None),
            P("fsdp", "tm", None),
            P("fsdp", "tm", None),
            P("fsdp", None),
            P("fsdp", None),
            P("tm", None, None),
            P("tm"),
        ),
        out_specs=(P("fsdp", "tm", None), P("fsdp", "tm", None), P("fsdp", "tm"), P("fsdp", "tm")),
        check_vma=False,
    )
```

```python
import jax
import jax.numpy as jnp
from jax import lax
from jax.experimental import pallas as pl
from jax.experimental.pallas import tpu as pltpu
from jax.sharding import PartitionSpec as P

H = 8
HS = 128
BLK = 128
TOK = 256
HD = 1024
D = 2048
MAXP = 8
BF = jnp.bfloat16
F32 = jnp.float32
MESH = pl.DeviceIdType.MESH
RING = 4
NZ = 8
NTM = RING * NZ
NF = 8
TILE = 256
AHEAD = 3
HALO = 384
SCALE = HS**-0.5
NN = (((1,), (0,)), ((), ()))
NT = (((1,), (1,)), ((), ()))
TN = (((0,), (0,)), ((), ()))


def mm(a, b, dims):
    return lax.dot_general(a, b, dims, preferred_element_type=F32)


class Place:
    def __init__(self):
        self.tm = lax.axis_index("tm")
        self.fsdp = lax.axis_index("fsdp")
        self.z, self.y = self.tm // RING, self.tm % RING
        self.x, self.core = self.fsdp // 2, self.fsdp % 2

    def at(self, x=None, core=None, z=None, y=None):
        x = self.x if x is None else x
        core = self.core if core is None else core
        z = self.z if z is None else z
        y = self.y if y is None else y
        return (z * RING + y, x * 2 + core)

    def step(self, axis, by):
        if axis == "x":
            return self.at(x=(self.x + by) % RING)
        if axis == "y":
            return self.at(y=(self.y + by) % RING)
        return self.at(z=(self.z + by) % NZ)

    def partner(self):
        return self.at(core=1 - self.core)

    def later(self, by):
        return ((self.tm + NTM + by) % NTM, self.fsdp)


def greet(devices):
    barrier = pltpu.get_barrier_semaphore()
    for device in devices:
        pl.semaphore_signal(barrier, inc=1, device_id=device, device_id_type=MESH)
    pl.semaphore_wait(barrier, len(devices))


def whole_kernel(
    x_hbm,
    q_hbm,
    k_hbm,
    v_hbm,
    do_hbm,
    wk_hbm,
    wv_hbm,
    pairs_ref,
    count_ref,
    dq_hbm,
    dx_hbm,
    key_ref,
    value_ref,
    q_ref,
    k_ref,
    v_ref,
    do_ref,
    dq,
    dx,
    bias,
    kwin,
    vwin,
    qwin,
    cwin,
    own,
    stat_send,
    stat_near,
    stat_far,
    wbuf,
    g,
    gts,
    xs,
    rings,
    finals,
    z_sends,
    z_recv,
    halo_sems,
    relay_sems,
    stat_sems,
    w_sems,
    x_sems,
    gt_sems,
    ring_sems,
    ring2_sems,
    z_sent,
    z_came,
    local_sems,
):
    here = Place()
    later, earlier, partner = here.later(1), here.later(-1), here.partner()
    earlier2 = here.later(-2)

    loads = [
        pltpu.make_async_copy(src, dst, local_sems.at[i])
        for i, (src, dst) in enumerate(
            ((k_hbm, k_ref), (q_hbm, q_ref), (v_hbm, v_ref), (do_hbm, do_ref))
        )
    ]
    own_rows = []
    for i, src in enumerate((wk_hbm, wv_hbm)):
        own_rows.append(pltpu.make_async_copy(src, wbuf.at[here.fsdp, i], local_sems.at[4 + i]))
    for xp in range(RING):
        columns = pl.ds(pl.multiple_of(xp * 512 + here.core * TILE, TILE), TILE)
        own_rows.append(pltpu.make_async_copy(x_hbm.at[:, columns], xs.at[0, xp], local_sems.at[6 + xp]))
    for copy in loads + own_rows:
        copy.start()

    greet(
        [partner, later, earlier, here.later(2), earlier2]
        + [here.step(axis, by) for axis in ("x", "y") for by in (1, 3)]
        + [here.step("z", by) for by in range(1, NZ)]
    )
    sent = []

    def remote(src, dst, sems, at, device):
        return pltpu.make_async_remote_copy(
            src_ref=src,
            dst_ref=dst,
            send_sem=sems.at[(0,) + at],
            recv_sem=sems.at[(1,) + at],
            device_id=device,
            device_id_type=MESH,
        )

    def send(src, dst, sems, at, device):
        copy = remote(src, dst, sems, at, device)
        copy.start()
        sent.append(copy)
        return copy

    def lanes(h):
        head = h // 4 + 4 * (h % 2) + 2 * ((h % 4) // 2)
        return pl.ds(pl.multiple_of(head * HS, HS), HS)

    streams = (
        (k_hbm, kwin, BLK, 2 * BLK, 0, later),
        (v_hbm, vwin, BLK, 2 * BLK, 0, later),
        (q_hbm, qwin, 0, 0, 2 * BLK, earlier),
        (do_hbm, cwin, 0, 0, 2 * BLK, earlier),
    )

    def halo(h):
        return [
            remote(ref.at[:, lanes(h)], win.at[h, pl.ds(at, TOK)], halo_sems, (i, h), device)
            for i, (ref, win, at, _, _, device) in enumerate(streams)
        ]

    def relay(h, which=range(4)):
        copies = []
        for i in which:
            _, win, _, src, dst, device = streams[i]
            copies.append(
                remote(win.at[h, pl.ds(src, BLK)], win.at[h, pl.ds(dst, BLK)], relay_sems, (i, h), device)
            )
        return copies

    def stats(h):
        return [
            remote(stat_send.at[h], stat_near.at[h], stat_sems, (0, h), earlier),
            remote(stat_send.at[h, :, pl.ds(0, BLK)], stat_far.at[h], stat_sems, (1, h), earlier2),
        ]

    starts = (0, 4, 6)

    def turned(h, group):
        rows = pl.ds(pl.multiple_of((h - starts[group]) * 32, 32), 32)
        gt = gts[group]
        return remote(gt.at[0, :, :, rows], gt.at[1, :, :, rows], gt_sems, (h,), partner)

    def start(copies):
        for copy in copies:
            copy.start()

    def arrive(copies):
        for copy in copies:
            copy.wait_recv()

    for h in range(AHEAD):
        start(halo(h))

    weights = (wk_hbm, wv_hbm)
    right, left = here.step("x", 1), here.step("x", 3)
    mine = here.fsdp
    left_id = ((here.x + 3) % RING) * 2 + here.core
    right_id = ((here.x + 1) % RING) * 2 + here.core
    opp_id = ((here.x + 2) % RING) * 2 + here.core
    from_left, from_right = {}, {}
    for i in (0, 1):
        from_left[i] = send(weights[i], wbuf.at[mine, i], w_sems, (i,), right)
        from_right[1 - i] = send(weights[1 - i], wbuf.at[mine, 1 - i], w_sems, (2 + 1 - i,), left)
    crossed = []
    for i in (0, 1):
        crossed.append(send(weights[i], wbuf.at[mine, i], w_sems, (6 + i,), partner))
    x_cross = []
    for xp in range(RING):
        theirs = pl.multiple_of(xp * 512 + (1 - here.core) * TILE, TILE)
        x_cross.append(send(x_hbm.at[:, pl.ds(theirs, TILE)], xs.at[1, xp], x_sems, (xp,), partner))

    def forward_weights():
        from_left[0].wait_recv()
        opp_k = send(wbuf.at[left_id, 0], wbuf.at[left_id, 0], w_sems, (4,), right)
        crossed.append(send(wbuf.at[left_id, 0], wbuf.at[left_id, 0], w_sems, (8,), partner))
        from_right[1].wait_recv()
        opp_v = send(wbuf.at[right_id, 1], wbuf.at[right_id, 1], w_sems, (5,), left)
        crossed.append(send(wbuf.at[right_id, 1], wbuf.at[right_id, 1], w_sems, (9,), partner))
        return opp_k, opp_v

    def cross_weights(opp_k, opp_v):
        from_left[1].wait_recv()
        crossed.append(send(wbuf.at[left_id, 1], wbuf.at[left_id, 1], w_sems, (10,), partner))
        from_right[0].wait_recv()
        crossed.append(send(wbuf.at[right_id, 0], wbuf.at[right_id, 0], w_sems, (11,), partner))
        opp_k.wait_recv()
        crossed.append(send(wbuf.at[opp_id, 0], wbuf.at[opp_id, 0], w_sems, (12,), partner))
        opp_v.wait_recv()
        crossed.append(send(wbuf.at[opp_id, 1], wbuf.at[opp_id, 1], w_sems, (13,), partner))

    key_at = lax.broadcasted_iota(jnp.int32, (BLK, BLK), 0)
    query_at = lax.broadcasted_iota(jnp.int32, (BLK, BLK), 1)
    levels = {}
    for qb in range(2):
        for kb in range(4):
            query_block = here.tm * 2 + qb
            key_block = query_block - 3 + kb
            hit = None
            for r in range(MAXP):
                same = (
                    (r < count_ref[0])
                    & (pairs_ref[0, r] == query_block)
                    & (pairs_ref[1, r] == key_block)
                )
                hit = same if hit is None else hit | same
            levels[qb, kb] = jnp.where(hit, 0.0, -jnp.inf)
            level = jnp.full((BLK, BLK), levels[qb, kb], F32)
            if kb == 3:
                level = jnp.where(key_at <= query_at, level, -jnp.inf)
            bias[qb, kb * BLK : (kb + 1) * BLK] = level
    rows = [
        jnp.concatenate([jnp.full((1, BLK), levels[0, a], F32), jnp.full((1, BLK), levels[1, b], F32)], axis=1)
        for a, b in ((1, 0), (2, 1), (0, 0))
    ]
    for h in range(H):
        for i, row in enumerate(rows):
            stat_send[h, 3 + i : 4 + i] = row

    def query_side(h):
        query, cotangent = q_ref[:, lanes(h)], do_ref[:, lanes(h)]
        keys = jnp.concatenate([kwin[h], k_ref[:, lanes(h)]], axis=0)
        values = jnp.concatenate([vwin[h], v_ref[:, lanes(h)]], axis=0)
        scores = mm(keys, query, NT)
        grad_probs = mm(values, cotangent, NT)
        probs_parts, grads_parts, noted = [], [], []
        for qb in range(2):
            near, columns = slice(qb * BLK, qb * BLK + 512), slice(qb * BLK, qb * BLK + BLK)
            score = scores[near, columns] * SCALE + bias[qb]
            most = jnp.max(score, axis=0, keepdims=True)
            prob = jnp.exp(score - most)
            share = 1.0 / jnp.sum(prob, axis=0, keepdims=True)
            prob = prob * share
            low = prob.astype(BF)
            grad = grad_probs[near, columns]
            row_dot = jnp.sum(low.astype(F32) * grad, axis=0, keepdims=True)
            probs_parts.append(low)
            grads_parts.append((prob * (grad - row_dot)).astype(BF))
            noted.append((most, share, row_dot))
        for i in range(3):
            stat_send[h, i : i + 1] = jnp.concatenate([noted[0][i], noted[1][i]], axis=1)
        start(stats(h))
        blank = jnp.zeros((BLK, BLK), BF)
        grads_low = jnp.concatenate(
            [
                jnp.concatenate([grads_parts[0], blank], axis=0),
                jnp.concatenate([blank, grads_parts[1]], axis=0),
            ],
            axis=1,
        )
        probs_own = jnp.concatenate(
            [jnp.concatenate([probs_parts[0][HALO:], blank], axis=0), probs_parts[1][2 * BLK :]],
            axis=1,
        )
        dq[:, lanes(h)] = (mm(grads_low, keys, TN) * SCALE).astype(BF)
        own[h % 2, 0] = mm(grads_low[HALO:], query, NN)
        own[h % 2, 1] = mm(probs_own, cotangent, NN)

    def key_side(h, group):
        arrive(relay(h, (2, 3)) + stats(h))
        query, cotangent = qwin[h], cwin[h]
        keys, values = k_ref[:, lanes(h)], v_ref[:, lanes(h)]
        scores = mm(keys, query, NT)
        grad_probs = mm(values, cotangent, NT)
        most, share, row_dot = (
            jnp.concatenate([stat_near[h, i : i + 1], stat_far[h, i : i + 1]], axis=1) for i in range(3)
        )
        never = jnp.full((1, BLK), -jnp.inf, F32)
        levels = (
            jnp.concatenate([stat_near[h, 3:4], never], axis=1),
            jnp.concatenate([stat_near[h, 4:5], stat_far[h, 5:6]], axis=1),
        )
        probs_parts, grads_parts = [], []
        for b in range(2):
            block = slice(b * BLK, b * BLK + BLK)
            prob = jnp.exp(scores[block] * SCALE + levels[b] - most) * share
            probs_parts.append(prob.astype(BF))
            grads_parts.append((prob * (grad_probs[block] - row_dot)).astype(BF))
        keys_grad = mm(jnp.concatenate(grads_parts, axis=0), query, NN)
        values_grad = mm(jnp.concatenate(probs_parts, axis=0), cotangent, NN)
        for i, full in enumerate(((own[h % 2, 0] + keys_grad) * SCALE, own[h % 2, 1] + values_grad)):
            low = full.astype(BF)
            g[i, :, lanes(h)] = low
            flipped = low.T
            rows = pl.ds(pl.multiple_of((h - starts[group]) * 32, 32), 32)
            for yp in range(RING):
                part = flipped[yp * 32 : yp * 32 + 32]
                if group == 2:
                    gts[2][0, i, yp, rows] = part
                else:
                    gts[group][0, yp, i, rows] = part
        turned(h, group).start()

    for copy in loads:
        copy.wait()
    arrive(halo(0))
    start(relay(0))

    axes = (("x", "y"), ("y", "x"), ("x", "y"), ("y", "x"))
    groups = (0, 1, 2, 2)
    heights = (256, 128, 64, 64)
    place = {"x": here.x, "y": here.y}
    slots = (2, 1, 3, 0)
    ways = (1, 3)
    opposite, beside, second, pieces = {}, {}, {}, {}

    def block(t, ring, slot):
        b = (place[axes[t][1]] + slots[slot]) % RING
        xp, yp = (b, ring) if axes[t][0] == "y" else (ring, b)
        terms = []
        for side in range(2):
            if t < 2:
                lhs = gts[t][side, yp].reshape(heights[t], TOK)
            else:
                lhs = gts[2][side, t - 2, yp]
            terms.append(mm(lhs, xs[side, xp], NN))
        return terms[0] + terms[1]

    def ring(t, d):
        return (place[axes[t][0]] + ways[d]) % RING

    def send_opposite(t):
        opp_send, opp_recv = rings[t][:2]
        opp = (place[axes[t][0]] + 2) % RING
        for i in range(2):
            for d in range(2):
                slot = 2 * d + i
                opp_send[slot] = block(t, opp, slot).astype(BF)
                opposite[t, slot] = send(
                    opp_send.at[slot],
                    opp_recv.at[slot],
                    ring_sems,
                    (t, slot),
                    here.step(axes[t][0], ways[d]),
                )

    def give(t, d, slot, value):
        nb_send, nb_recv = rings[t][2:4]
        nb_send[d, slot] = value.astype(BF)
        beside[t, d, slot] = send(
            nb_send.at[d, slot],
            nb_recv.at[d, slot],
            ring_sems,
            (t, 4 + d * 4 + slot),
            here.step(axes[t][0], ways[d]),
        )

    def send_free(t):
        for i in range(2):
            for d in range(2):
                slot = 2 * (1 - d) + i
                give(t, d, slot, block(t, ring(t, d), slot))

    def send_bound(t):
        opp_recv = rings[t][1]
        order = [(d, 2 * d + i) for i in range(2) for d in range(2)]
        made = [block(t, ring(t, d), slot) for d, slot in order]
        for (d, slot), value in zip(order, made):
            opposite[t, slot].wait_recv()
            give(t, d, slot, value + opp_recv[slot].astype(F32))

    def total(t, slot, value):
        nb_recv = rings[t][3]
        for d in range(2):
            beside[t, d, slot].wait_recv()
        return value + nb_recv[0, slot].astype(F32) + nb_recv[1, slot].astype(F32)

    def give2(t, d, half, value):
        nb2_send, nb2_recv = rings[t][6:8]
        height = heights[t] // 2
        part = pl.ds(height * half, height)
        nb2_send[d, part] = value.astype(BF)
        pieces[t, d, half] = send(
            nb2_send.at[d, part],
            nb2_recv.at[d, part],
            ring2_sems,
            (t, 2 + 2 * d + half),
            here.step(axes[t][1], ways[d]),
        )

    def open_second(t):
        opp2_send, opp2_recv = rings[t][4:6]
        sums = rings[t][8]
        height = heights[t] // 2
        made = [block(t, place[axes[t][0]], slot) for slot in range(4)]
        opp2_send[...] = total(t, 0, made[0]).astype(BF)
        for d in range(2):
            second[t, d] = send(
                opp2_send.at[pl.ds(height * d, height)],
                opp2_recv.at[d],
                ring2_sems,
                (t, d),
                here.step(axes[t][1], ways[d]),
            )
        for d in range(2):
            sums[d] = total(t, 1 + d, made[1 + d])
            give2(t, d, 1 - d, sums[d, pl.ds(height * (1 - d), height)])
        sums[2] = total(t, 3, made[3])

    def bound_second(t):
        opp2_recv, sums = rings[t][5], rings[t][8]
        height = heights[t] // 2
        for d in range(2):
            second[t, d].wait_recv()
            give2(t, d, d, sums[d, pl.ds(height * d, height)] + opp2_recv[d].astype(F32))

    def owner(t, p):
        return (4 * (p % 2) + 2 * (p // 2), 1 + 4 * p, 3 + 4 * p)[groups[t]]

    def z_copy(t, p):
        by = (owner(t, p) - here.z + NZ) % NZ
        at, there = (p,), (by,)
        if t > 1:
            at, there = at + (t - 2,), there + (t - 2,)
        copy = pltpu.make_async_remote_copy(
            src_ref=z_sends[groups[t]].at[at],
            dst_ref=z_recv.at[there],
            send_sem=z_sent.at[t, p],
            recv_sem=z_came.at[max(t - 2, 0), by],
            device_id=here.at(z=owner(t, p)),
            device_id_type=MESH,
        )
        return by, copy

    counts = (4, 2, 2)

    def finish(t):
        nb2_recv, sums = rings[t][7], rings[t][8]
        for d in range(2):
            for half in range(2):
                pieces[t, d, half].wait_recv()
        whole = sums[2] + nb2_recv[0].astype(F32) + nb2_recv[1].astype(F32)
        count = counts[groups[t]]
        for i, half in enumerate((0, 1) if t < 2 else (t - 2,)):
            for p in range(count):
                part = whole[(i * count + p) * 32 : (i * count + p) * 32 + 32]
                finals[groups[t]][p, half] = part
                z_sends[groups[t]][p, half] = part.astype(BF)
        for p in range(count):
            by, copy = z_copy(t, p)

            @pl.when(by != 0)
            def _():
                copy.start()

    def input_rows(f, carry):
        columns = pl.ds(pl.multiple_of(f * TILE, TILE), TILE)
        dx[:, columns] = (mm(g[0], wbuf[f, 0], NT) + mm(g[1], wbuf[f, 1], NT)).astype(BF)
        return carry

    def body(h, carry, group=0, first=False, more=True, last=False, between=None):
        if more:
            start(halo(h + AHEAD))
        if not last:
            arrive(halo(h + 1))
            start(relay(h + 1))
        arrive(relay(h, (0, 1)))
        query_side(h)
        if between is not None:
            between()
        if not first:
            key_side(h - 1, group)
        return carry

    body(0, 0, first=True)
    lax.fori_loop(1, 4, body, 0)
    opp_weights = forward_weights()
    body(4, 0)

    def open_first():
        for copy in own_rows:
            copy.wait()
        arrive(x_cross + [turned(h, 0) for h in range(4)])
        send_opposite(0)

    def open_next():
        arrive([turned(h, 1) for h in (4, 5)])
        send_opposite(1)

    body(5, 0, group=1, more=False, between=open_first)
    send_free(0)
    body(6, 0, group=1, more=False)
    body(7, 0, group=2, more=False, last=True, between=open_next)
    send_bound(0)
    send_free(1)
    key_side(7, 2)
    dq_out = pltpu.make_async_copy(dq, dq_hbm, local_sems.at[10])
    dq_out.start()
    send_bound(1)
    arrive([turned(h, 2) for h in (6, 7)])
    for t in (2, 3):
        send_opposite(t)
    for t in (2, 3):
        send_free(t)
    open_second(0)
    for t in (2, 3):
        send_bound(t)
    def drain(h, carry):
        for copy in halo(h) + relay(h) + stats(h):
            copy.wait_send()
        return carry

    lax.fori_loop(0, H, drain, 0)
    for h in range(H):
        turned(h, (h > 3) + (h > 5)).wait_send()
    for copy in sent:
        copy.wait_send()
    sent.clear()
    bound_second(0)
    cross_weights(*opp_weights)
    open_second(1)
    finish(0)
    arrive(crossed)
    lax.fori_loop(0, 3, input_rows, 0)
    for t in (2, 3):
        open_second(t)
    bound_second(1)
    lax.fori_loop(3, 5, input_rows, 0)
    for t in (2, 3):
        bound_second(t)
    finish(1)
    lax.fori_loop(5, 7, input_rows, 0)
    for t in (2, 3):
        finish(t)
    lax.fori_loop(7, NF, input_rows, 0)
    dx_out = pltpu.make_async_copy(dx, dx_hbm, local_sems.at[11])
    dx_out.start()

    def gather(group, p, halves):
        for half in range(halves):
            for by in range(1, NZ):
                at, there = ((p,), (by,)) if halves == 1 else ((p, half), (by, half))
                pltpu.make_async_remote_copy(
                    src_ref=z_sends[group].at[at],
                    dst_ref=z_recv.at[there],
                    send_sem=z_sent.at[0, 0],
                    recv_sem=z_came.at[half, by],
                    device_id=here.step("z", by),
                    device_id_type=MESH,
                ).wait_recv()
        for half, out_ref in enumerate((key_ref, value_ref)):
            whole = finals[group][p, half]
            for by in range(1, NZ):
                whole = whole + z_recv[by, half].astype(F32)
            out_ref[...] = whole

    @pl.when(here.z % 2 == 0)
    def _():
        gather(0, here.z // 4 + 2 * ((here.z % 4) // 2), 1)

    @pl.when(here.z % 4 == 1)
    def _():
        gather(1, here.z // 4, 1)

    @pl.when(here.z % 4 == 3)
    def _():
        gather(2, here.z // 4, 2)

    dq_out.wait()
    dx_out.wait()
    for copy in sent:
        copy.wait_send()
    for t in range(4):
        for p in range(counts[groups[t]]):
            by, copy = z_copy(t, p)

            @pl.when(by != 0)
            def _():
                copy.wait_send()


def hand_over(*refs):
    count = (len(refs) - 1) // 2
    copies = [
        pltpu.make_async_copy(refs[i], refs[count + i], refs[-1].at[i]) for i in range(count)
    ]
    for copy in copies:
        copy.start()
    for copy in copies:
        copy.wait()


def shards(
    inputs,
    query_rows,
    saved_key_rows,
    value_rows,
    grad_out,
    key_weight,
    value_weight,
    block_pairs,
    pair_counts,
):
    vmem = pl.BlockSpec(memory_space=pltpu.VMEM)
    smem = pl.BlockSpec(memory_space=pltpu.SMEM)
    anywhere = pl.BlockSpec(memory_space=pl.ANY)
    shapes = [
        jax.ShapeDtypeStruct((TOK, HD), BF),
        jax.ShapeDtypeStruct((TOK, D), BF),
        jax.ShapeDtypeStruct((32, TILE), F32),
        jax.ShapeDtypeStruct((32, TILE), F32),
    ]
    made = pl.pallas_call(
        whole_kernel,
        out_shape=shapes,
        in_specs=[anywhere] * 7 + [smem] * 2,
        out_specs=[anywhere] * 2 + [vmem] * 2,
        scratch_shapes=[
            pltpu.VMEM((TOK, HD), BF),
            pltpu.VMEM((TOK, HD), BF),
            pltpu.VMEM((TOK, HD), BF),
            pltpu.VMEM((TOK, HD), BF),
            pltpu.VMEM((TOK, HD), BF),
            pltpu.VMEM((TOK, D), BF),
            pltpu.VMEM((2, 512, BLK), F32),
            pltpu.VMEM((H, HALO, HS), BF),
            pltpu.VMEM((H, HALO, HS), BF),
            pltpu.VMEM((H, HALO, HS), BF),
            pltpu.VMEM((H, HALO, HS), BF),
            pltpu.VMEM((2, 2, TOK, HS), F32),
            pltpu.VMEM((H, 8, TOK), F32),
            pltpu.VMEM((H, 8, TOK), F32),
            pltpu.VMEM((H, 8, BLK), F32),
            pltpu.VMEM((NF, 2, TILE, HD), BF),
            pltpu.VMEM((2, TOK, HD), BF),
            [
                pltpu.VMEM((2, RING, 2, 128, TOK), BF),
                pltpu.VMEM((2, RING, 2, 64, TOK), BF),
                pltpu.VMEM((2, 2, RING, 64, TOK), BF),
            ],
            pltpu.VMEM((2, RING, TOK, TILE), BF),
            [
                [
                    pltpu.VMEM((4, height, TILE), BF),
                    pltpu.VMEM((4, height, TILE), BF),
                    pltpu.VMEM((2, 4, height, TILE), BF),
                    pltpu.VMEM((2, 4, height, TILE), BF),
                    pltpu.VMEM((height, TILE), BF),
                    pltpu.VMEM((2, height // 2, TILE), BF),
                    pltpu.VMEM((2, height, TILE), BF),
                    pltpu.VMEM((2, height, TILE), BF),
                    pltpu.VMEM((3, height, TILE), F32),
                ]
                for height in (256, 128, 64, 64)
            ],
            [pltpu.VMEM((count, 2, 32, TILE), F32) for count in (4, 2, 2)],
            [pltpu.VMEM((count, 2, 32, TILE), BF) for count in (4, 2, 2)],
            pltpu.VMEM((NZ, 2, 32, TILE), BF),
            pltpu.SemaphoreType.DMA((2, 4, H)),
            pltpu.SemaphoreType.DMA((2, 4, H)),
            pltpu.SemaphoreType.DMA((2, 2, H)),
            pltpu.SemaphoreType.DMA((2, 14)),
            pltpu.SemaphoreType.DMA((2, RING)),
            pltpu.SemaphoreType.DMA((2, H)),
            pltpu.SemaphoreType.DMA((2, 4, 12)),
            pltpu.SemaphoreType.DMA((2, 4, 6)),
            pltpu.SemaphoreType.DMA((4, 4)),
            pltpu.SemaphoreType.DMA((2, NZ)),
            pltpu.SemaphoreType.DMA((12,)),
        ],
        compiler_params=pltpu.CompilerParams(
            collective_id=0, has_side_effects=True, vmem_limit_bytes=56 * 1024 * 1024
        ),
    )(
        inputs[0],
        query_rows[0],
        saved_key_rows[0],
        value_rows[0],
        grad_out[0],
        key_weight,
        value_weight,
        block_pairs[0].T,
        pair_counts,
    )
    grad_query, input_gradient, key_total, value_total = pl.pallas_call(
        hand_over,
        out_shape=shapes,
        in_specs=[vmem] * 4,
        out_specs=[anywhere] * 4,
        scratch_shapes=[pltpu.SemaphoreType.DMA((4,))],
    )(*made)
    return (grad_query[None], input_gradient[None], key_total.T, value_total.T)


def solution(mesh):
    return jax.shard_map(
        shards,
        mesh=mesh,
        in_specs=(
            P("fsdp", "tm", None),
            P("fsdp", "tm", None),
            P("fsdp", "tm", None),
            P("fsdp", "tm", None),
            P("fsdp", "tm", None),
            P("fsdp", None),
            P("fsdp", None),
            P("tm", None, None),
            P("tm"),
        ),
        out_specs=(P("fsdp", "tm", None), P("fsdp", "tm", None), P("fsdp", "tm"), P("fsdp", "tm")),
        check_vma=False,
    )
```

```python
import jax
import jax.numpy as jnp
from jax import lax
from jax.experimental import pallas as pl
from jax.experimental.pallas import tpu as pltpu
from jax.sharding import PartitionSpec as P

H = 8
HS = 128
BLK = 128
TOK = 256
HD = 1024
D = 2048
MAXP = 8
BF = jnp.bfloat16
F32 = jnp.float32
MESH = pl.DeviceIdType.MESH
RING = 4
NZ = 8
NTM = RING * NZ
NF = 8
TILE = 256
AHEAD = 3
HALO = 384
SCALE = HS**-0.5
NN = (((1,), (0,)), ((), ()))
NT = (((1,), (1,)), ((), ()))
TN = (((0,), (0,)), ((), ()))


def mm(a, b, dims):
    return lax.dot_general(a, b, dims, preferred_element_type=F32)


class Place:
    def __init__(self):
        self.tm = lax.axis_index("tm")
        self.fsdp = lax.axis_index("fsdp")
        self.z, self.y = self.tm // RING, self.tm % RING
        self.x, self.core = self.fsdp // 2, self.fsdp % 2

    def at(self, x=None, core=None, z=None, y=None):
        x = self.x if x is None else x
        core = self.core if core is None else core
        z = self.z if z is None else z
        y = self.y if y is None else y
        return (z * RING + y, x * 2 + core)

    def step(self, axis, by):
        if axis == "x":
            return self.at(x=(self.x + by) % RING)
        if axis == "y":
            return self.at(y=(self.y + by) % RING)
        return self.at(z=(self.z + by) % NZ)

    def partner(self):
        return self.at(core=1 - self.core)

    def later(self, by):
        return ((self.tm + NTM + by) % NTM, self.fsdp)


def greet(devices):
    barrier = pltpu.get_barrier_semaphore()
    for device in devices:
        pl.semaphore_signal(barrier, inc=1, device_id=device, device_id_type=MESH)
    pl.semaphore_wait(barrier, len(devices))


def whole_kernel(
    x_hbm,
    q_hbm,
    k_hbm,
    v_hbm,
    do_hbm,
    wk_hbm,
    wv_hbm,
    pairs_ref,
    count_ref,
    dq_hbm,
    dx_hbm,
    key_ref,
    value_ref,
    q_ref,
    k_ref,
    v_ref,
    do_ref,
    dq,
    dx,
    bias,
    kwin,
    vwin,
    qwin,
    cwin,
    own,
    stat_send,
    stat_near,
    stat_far,
    wbuf,
    g,
    gts,
    xs,
    rings,
    finals,
    z_sends,
    z_recv,
    halo_sems,
    relay_sems,
    stat_sems,
    w_sems,
    x_sems,
    gt_sems,
    ring_sems,
    ring2_sems,
    z_sent,
    z_came,
    local_sems,
):
    here = Place()
    later, earlier, partner = here.later(1), here.later(-1), here.partner()
    earlier2 = here.later(-2)

    loads = [
        pltpu.make_async_copy(src, dst, local_sems.at[i])
        for i, (src, dst) in enumerate(
            ((k_hbm, k_ref), (q_hbm, q_ref), (v_hbm, v_ref), (do_hbm, do_ref))
        )
    ]
    own_rows = []
    for i, src in enumerate((wk_hbm, wv_hbm)):
        own_rows.append(pltpu.make_async_copy(src, wbuf.at[here.fsdp, i], local_sems.at[4 + i]))
    for xp in range(RING):
        columns = pl.ds(pl.multiple_of(xp * 512 + here.core * TILE, TILE), TILE)
        own_rows.append(pltpu.make_async_copy(x_hbm.at[:, columns], xs.at[0, xp], local_sems.at[6 + xp]))
    for copy in loads + own_rows:
        copy.start()

    greet(
        [partner, later, earlier, here.later(2), earlier2]
        + [here.step(axis, by) for axis in ("x", "y") for by in (1, 3)]
        + [here.step("x", 2), here.step("y", 2)]
        + [here.step("z", by) for by in range(1, NZ)]
    )
    sent = []

    def remote(src, dst, sems, at, device):
        return pltpu.make_async_remote_copy(
            src_ref=src,
            dst_ref=dst,
            send_sem=sems.at[(0,) + at],
            recv_sem=sems.at[(1,) + at],
            device_id=device,
            device_id_type=MESH,
        )

    def send(src, dst, sems, at, device):
        copy = remote(src, dst, sems, at, device)
        copy.start()
        sent.append(copy)
        return copy

    def lanes(h):
        head = h // 4 + 4 * (h % 2) + 2 * ((h % 4) // 2)
        return pl.ds(pl.multiple_of(head * HS, HS), HS)

    streams = (
        (k_hbm, kwin, BLK, 2 * BLK, 0, later),
        (v_hbm, vwin, BLK, 2 * BLK, 0, later),
        (q_hbm, qwin, 0, 0, 2 * BLK, earlier),
        (do_hbm, cwin, 0, 0, 2 * BLK, earlier),
    )

    def halo(h):
        return [
            remote(ref.at[:, lanes(h)], win.at[h, pl.ds(at, TOK)], halo_sems, (i, h), device)
            for i, (ref, win, at, _, _, device) in enumerate(streams)
        ]

    def relay(h, which=range(4)):
        copies = []
        for i in which:
            _, win, _, src, dst, device = streams[i]
            copies.append(
                remote(win.at[h, pl.ds(src, BLK)], win.at[h, pl.ds(dst, BLK)], relay_sems, (i, h), device)
            )
        return copies

    def stats(h):
        return [
            remote(stat_send.at[h], stat_near.at[h], stat_sems, (0, h), earlier),
            remote(stat_send.at[h, :, pl.ds(0, BLK)], stat_far.at[h], stat_sems, (1, h), earlier2),
        ]

    starts = (0, 4, 6)

    def turned(h, group):
        rows = pl.ds(pl.multiple_of((h - starts[group]) * 32, 32), 32)
        gt = gts[group]
        return remote(gt.at[0, :, :, rows], gt.at[1, :, :, rows], gt_sems, (h,), partner)

    def start(copies):
        for copy in copies:
            copy.start()

    def arrive(copies):
        for copy in copies:
            copy.wait_recv()

    for h in range(AHEAD):
        start(halo(h))

    weights = (wk_hbm, wv_hbm)
    right, left = here.step("x", 1), here.step("x", 3)
    mine = here.fsdp
    left_id = ((here.x + 3) % RING) * 2 + here.core
    right_id = ((here.x + 1) % RING) * 2 + here.core
    opp_id = ((here.x + 2) % RING) * 2 + here.core
    from_left, from_right = {}, {}
    for i in (0, 1):
        from_left[i] = send(weights[i], wbuf.at[mine, i], w_sems, (i,), right)
        from_right[1 - i] = send(weights[1 - i], wbuf.at[mine, 1 - i], w_sems, (2 + 1 - i,), left)
    crossed = []
    for i in (0, 1):
        crossed.append(send(weights[i], wbuf.at[mine, i], w_sems, (6 + i,), partner))
    x_cross = []
    for xp in range(RING):
        theirs = pl.multiple_of(xp * 512 + (1 - here.core) * TILE, TILE)
        x_cross.append(send(x_hbm.at[:, pl.ds(theirs, TILE)], xs.at[1, xp], x_sems, (xp,), partner))

    def forward_weights():
        from_left[0].wait_recv()
        opp_k = send(wbuf.at[left_id, 0], wbuf.at[left_id, 0], w_sems, (4,), right)
        crossed.append(send(wbuf.at[left_id, 0], wbuf.at[left_id, 0], w_sems, (8,), partner))
        from_right[1].wait_recv()
        opp_v = send(wbuf.at[right_id, 1], wbuf.at[right_id, 1], w_sems, (5,), left)
        crossed.append(send(wbuf.at[right_id, 1], wbuf.at[right_id, 1], w_sems, (9,), partner))
        return opp_k, opp_v

    def cross_weights(opp_k, opp_v):
        from_left[1].wait_recv()
        crossed.append(send(wbuf.at[left_id, 1], wbuf.at[left_id, 1], w_sems, (10,), partner))
        from_right[0].wait_recv()
        crossed.append(send(wbuf.at[right_id, 0], wbuf.at[right_id, 0], w_sems, (11,), partner))
        opp_k.wait_recv()
        crossed.append(send(wbuf.at[opp_id, 0], wbuf.at[opp_id, 0], w_sems, (12,), partner))
        opp_v.wait_recv()
        crossed.append(send(wbuf.at[opp_id, 1], wbuf.at[opp_id, 1], w_sems, (13,), partner))

    key_at = lax.broadcasted_iota(jnp.int32, (BLK, BLK), 0)
    query_at = lax.broadcasted_iota(jnp.int32, (BLK, BLK), 1)
    levels = {}
    for qb in range(2):
        for kb in range(4):
            query_block = here.tm * 2 + qb
            key_block = query_block - 3 + kb
            hit = None
            for r in range(MAXP):
                same = (
                    (r < count_ref[0])
                    & (pairs_ref[0, r] == query_block)
                    & (pairs_ref[1, r] == key_block)
                )
                hit = same if hit is None else hit | same
            levels[qb, kb] = jnp.where(hit, 0.0, -jnp.inf)
            level = jnp.full((BLK, BLK), levels[qb, kb], F32)
            if kb == 3:
                level = jnp.where(key_at <= query_at, level, -jnp.inf)
            bias[qb, kb * BLK : (kb + 1) * BLK] = level
    rows = [
        jnp.concatenate([jnp.full((1, BLK), levels[0, a], F32), jnp.full((1, BLK), levels[1, b], F32)], axis=1)
        for a, b in ((1, 0), (2, 1), (0, 0))
    ]
    for h in range(H):
        for i, row in enumerate(rows):
            stat_send[h, 3 + i : 4 + i] = row

    def query_side(h):
        query, cotangent = q_ref[:, lanes(h)], do_ref[:, lanes(h)]
        keys = jnp.concatenate([kwin[h], k_ref[:, lanes(h)]], axis=0)
        values = jnp.concatenate([vwin[h], v_ref[:, lanes(h)]], axis=0)
        scores = mm(keys, query, NT)
        grad_probs = mm(values, cotangent, NT)
        probs_parts, grads_parts, noted = [], [], []
        for qb in range(2):
            near, columns = slice(qb * BLK, qb * BLK + 512), slice(qb * BLK, qb * BLK + BLK)
            score = scores[near, columns] * SCALE + bias[qb]
            most = jnp.max(score, axis=0, keepdims=True)
            prob = jnp.exp(score - most)
            share = 1.0 / jnp.sum(prob, axis=0, keepdims=True)
            prob = prob * share
            low = prob.astype(BF)
            grad = grad_probs[near, columns]
            row_dot = jnp.sum(low.astype(F32) * grad, axis=0, keepdims=True)
            probs_parts.append(low)
            grads_parts.append((prob * (grad - row_dot)).astype(BF))
            noted.append((most, share, row_dot))
        for i in range(3):
            stat_send[h, i : i + 1] = jnp.concatenate([noted[0][i], noted[1][i]], axis=1)
        start(stats(h))
        blank = jnp.zeros((BLK, BLK), BF)
        grads_low = jnp.concatenate(
            [
                jnp.concatenate([grads_parts[0], blank], axis=0),
                jnp.concatenate([blank, grads_parts[1]], axis=0),
            ],
            axis=1,
        )
        probs_own = jnp.concatenate(
            [jnp.concatenate([probs_parts[0][HALO:], blank], axis=0), probs_parts[1][2 * BLK :]],
            axis=1,
        )
        dq[:, lanes(h)] = (mm(grads_low, keys, TN) * SCALE).astype(BF)
        own[h % 2, 0] = mm(grads_low[HALO:], query, NN)
        own[h % 2, 1] = mm(probs_own, cotangent, NN)

    def key_side(h, group):
        arrive(relay(h, (2, 3)) + stats(h))
        query, cotangent = qwin[h], cwin[h]
        keys, values = k_ref[:, lanes(h)], v_ref[:, lanes(h)]
        scores = mm(keys, query, NT)
        grad_probs = mm(values, cotangent, NT)
        most, share, row_dot = (
            jnp.concatenate([stat_near[h, i : i + 1], stat_far[h, i : i + 1]], axis=1) for i in range(3)
        )
        never = jnp.full((1, BLK), -jnp.inf, F32)
        levels = (
            jnp.concatenate([stat_near[h, 3:4], never], axis=1),
            jnp.concatenate([stat_near[h, 4:5], stat_far[h, 5:6]], axis=1),
        )
        probs_parts, grads_parts = [], []
        for b in range(2):
            block = slice(b * BLK, b * BLK + BLK)
            prob = jnp.exp(scores[block] * SCALE + levels[b] - most) * share
            probs_parts.append(prob.astype(BF))
            grads_parts.append((prob * (grad_probs[block] - row_dot)).astype(BF))
        keys_grad = mm(jnp.concatenate(grads_parts, axis=0), query, NN)
        values_grad = mm(jnp.concatenate(probs_parts, axis=0), cotangent, NN)
        for i, full in enumerate(((own[h % 2, 0] + keys_grad) * SCALE, own[h % 2, 1] + values_grad)):
            low = full.astype(BF)
            g[i, :, lanes(h)] = low
            flipped = low.T
            rows = pl.ds(pl.multiple_of((h - starts[group]) * 32, 32), 32)
            for yp in range(RING):
                part = flipped[yp * 32 : yp * 32 + 32]
                if group == 2:
                    gts[2][0, i, yp, rows] = part
                else:
                    gts[group][0, yp, i, rows] = part
        turned(h, group).start()

    def pass_on(h):
        for near, onward in zip(halo(h), relay(h)):
            near.wait_recv()
            onward.start()

    for copy in loads:
        copy.wait()
    pass_on(0)

    axes = (("x", "y"), ("y", "x"), ("x", "y"), ("y", "x"))
    groups = (0, 1, 2, 2)
    heights = (256, 128, 64, 64)
    place = {"x": here.x, "y": here.y}
    slots = (2, 1, 3, 0)
    ways = (1, 3)
    opposite, beside, second, pieces = {}, {}, {}, {}

    def block(t, ring, slot):
        b = (place[axes[t][1]] + slots[slot]) % RING
        xp, yp = (b, ring) if axes[t][0] == "y" else (ring, b)
        terms = []
        for side in range(2):
            if t < 2:
                lhs = gts[t][side, yp].reshape(heights[t], TOK)
            else:
                lhs = gts[2][side, t - 2, yp]
            terms.append(mm(lhs, xs[side, xp], NN))
        return terms[0] + terms[1]

    def ring(t, d):
        return (place[axes[t][0]] + ways[d]) % RING

    def send_opposite(t):
        opp_send, opp_recv = rings[t][:2]
        opp = (place[axes[t][0]] + 2) % RING
        for i in range(2):
            for d in range(2):
                slot = 2 * d + i
                opp_send[slot] = block(t, opp, slot).astype(BF)
                opposite[t, slot] = send(
                    opp_send.at[slot],
                    opp_recv.at[slot],
                    ring_sems,
                    (t, slot),
                    here.step(axes[t][0], ways[d]),
                )

    def give(t, d, slot, value):
        nb_send, nb_recv = rings[t][2:4]
        nb_send[d, slot] = value.astype(BF)
        beside[t, d, slot] = send(
            nb_send.at[d, slot],
            nb_recv.at[d, slot],
            ring_sems,
            (t, 4 + d * 4 + slot),
            here.step(axes[t][0], ways[d]),
        )

    def send_free(t):
        for i in range(2):
            for d in range(2):
                slot = 2 * (1 - d) + i
                give(t, d, slot, block(t, ring(t, d), slot))

    def send_bound(t):
        opp_recv = rings[t][1]
        order = [(d, 2 * d + i) for i in range(2) for d in range(2)]
        made = [block(t, ring(t, d), slot) for d, slot in order]
        for (d, slot), value in zip(order, made):
            opposite[t, slot].wait_recv()
            give(t, d, slot, value + opp_recv[slot].astype(F32))

    def total(t, slot, value):
        nb_recv = rings[t][3]
        for d in range(2):
            beside[t, d, slot].wait_recv()
        return value + nb_recv[0, slot].astype(F32) + nb_recv[1, slot].astype(F32)

    def give2(t, d, half, value):
        nb2_send, nb2_recv = rings[t][6:8]
        height = heights[t] // 2
        part = pl.ds(height * half, height)
        nb2_send[d, part] = value.astype(BF)
        pieces[t, d, half] = send(
            nb2_send.at[d, part],
            nb2_recv.at[d, part],
            ring2_sems,
            (t, 2 + 2 * d + half),
            here.step(axes[t][1], ways[d]),
        )

    def open_second(t):
        opp2_send, opp2_recv = rings[t][4:6]
        sums = rings[t][8]
        height = heights[t] // 2
        made = [block(t, place[axes[t][0]], slot) for slot in range(4)]
        opp2_send[...] = total(t, 0, made[0]).astype(BF)
        for d in range(2):
            second[t, d] = send(
                opp2_send.at[pl.ds(height * d, height)],
                opp2_recv.at[d],
                ring2_sems,
                (t, d),
                here.step(axes[t][1], 2 if t > 1 else ways[d]),
            )
        for d in range(2):
            sums[d] = total(t, 1 + d, made[1 + d])
            give2(t, d, 1 - d, sums[d, pl.ds(height * (1 - d), height)])
            if t > 1:
                give2(t, d, d, sums[d, pl.ds(height * d, height)])
        sums[2] = total(t, 3, made[3])

    def bound_second(t):
        opp2_recv, sums = rings[t][5], rings[t][8]
        height = heights[t] // 2
        for d in range(2):
            second[t, d].wait_recv()
            give2(t, d, d, sums[d, pl.ds(height * d, height)] + opp2_recv[d].astype(F32))

    def owner(t, p):
        return (4 * (p % 2) + 2 * (p // 2), 1 + 4 * p, 3 + 4 * p)[groups[t]]

    def z_copy(t, p):
        by = (owner(t, p) - here.z + NZ) % NZ
        at, there = (p,), (by,)
        if t > 1:
            at, there = at + (t - 2,), there + (t - 2,)
        copy = pltpu.make_async_remote_copy(
            src_ref=z_sends[groups[t]].at[at],
            dst_ref=z_recv.at[there],
            send_sem=z_sent.at[t, p],
            recv_sem=z_came.at[max(t - 2, 0), by],
            device_id=here.at(z=owner(t, p)),
            device_id_type=MESH,
        )
        return by, copy

    counts = (4, 2, 2)

    def finish(t):
        nb2_recv, sums = rings[t][7], rings[t][8]
        for d in range(2):
            for half in range(2):
                pieces[t, d, half].wait_recv()
        whole = sums[2] + nb2_recv[0].astype(F32) + nb2_recv[1].astype(F32)
        if t > 1:
            for d in range(2):
                second[t, d].wait_recv()
            whole = whole + rings[t][5][...].reshape(heights[t], TILE).astype(F32)
        count = counts[groups[t]]
        for i, half in enumerate((0, 1) if t < 2 else (t - 2,)):
            for p in range(count):
                part = whole[(i * count + p) * 32 : (i * count + p) * 32 + 32]
                finals[groups[t]][p, half] = part
                z_sends[groups[t]][p, half] = part.astype(BF)
        for p in range(count):
            by, copy = z_copy(t, p)

            @pl.when(by != 0)
            def _():
                copy.start()

    def input_rows(f, carry):
        columns = pl.ds(pl.multiple_of(f * TILE, TILE), TILE)
        dx[:, columns] = (mm(g[0], wbuf[f, 0], NT) + mm(g[1], wbuf[f, 1], NT)).astype(BF)
        return carry

    def body(h, carry, group=0, first=False, more=True, last=False, before=None):
        if more:
            start(halo(h + AHEAD))
        if not last:
            pass_on(h + 1)
        if before is not None:
            before()
        arrive(relay(h, (0, 1)))
        query_side(h)
        if not first:
            key_side(h - 1, group)
        return carry

    body(0, 0, first=True)
    lax.fori_loop(1, 3, body, 0)
    opp_weights = forward_weights()
    body(3, 0)
    body(4, 0)

    def open_first():
        for copy in own_rows:
            copy.wait()
        arrive(x_cross + [turned(h, 0) for h in range(4)])
        send_opposite(0)

    def open_next():
        send_bound(0)
        arrive([turned(h, 1) for h in (4, 5)])
        send_opposite(1)

    body(5, 0, group=1, more=False, before=open_first)
    body(6, 0, group=1, more=False, before=lambda: send_free(0))
    body(7, 0, group=2, more=False, last=True, before=open_next)
    send_free(1)
    key_side(7, 2)
    dq_out = pltpu.make_async_copy(dq, dq_hbm, local_sems.at[10])
    dq_out.start()
    send_bound(1)
    arrive([turned(h, 2) for h in (6, 7)])
    for t in (2, 3):
        send_opposite(t)
    for t in (2, 3):
        send_free(t)
    open_second(0)
    for t in (2, 3):
        send_bound(t)
    def drain(h, carry):
        for copy in halo(h) + relay(h) + stats(h):
            copy.wait_send()
        return carry

    lax.fori_loop(0, H, drain, 0)
    for h in range(H):
        turned(h, (h > 3) + (h > 5)).wait_send()
    for copy in sent:
        copy.wait_send()
    sent.clear()
    bound_second(0)
    cross_weights(*opp_weights)
    open_second(1)
    finish(0)
    arrive(crossed)
    lax.fori_loop(0, 1, input_rows, 0)
    for t in (2, 3):
        open_second(t)
    bound_second(1)
    lax.fori_loop(1, 3, input_rows, 0)
    finish(1)
    lax.fori_loop(3, 5, input_rows, 0)
    for t in (2, 3):
        finish(t)
    lax.fori_loop(5, NF, input_rows, 0)
    dx_out = pltpu.make_async_copy(dx, dx_hbm, local_sems.at[11])
    dx_out.start()

    def gather(group, p, halves):
        for half in range(halves):
            for by in range(1, NZ):
                at, there = ((p,), (by,)) if halves == 1 else ((p, half), (by, half))
                pltpu.make_async_remote_copy(
                    src_ref=z_sends[group].at[at],
                    dst_ref=z_recv.at[there],
                    send_sem=z_sent.at[0, 0],
                    recv_sem=z_came.at[half, by],
                    device_id=here.step("z", by),
                    device_id_type=MESH,
                ).wait_recv()
        for half, out_ref in enumerate((key_ref, value_ref)):
            whole = finals[group][p, half]
            for by in range(1, NZ):
                whole = whole + z_recv[by, half].astype(F32)
            out_ref[...] = whole

    @pl.when(here.z % 2 == 0)
    def _():
        gather(0, here.z // 4 + 2 * ((here.z % 4) // 2), 1)

    @pl.when(here.z % 4 == 1)
    def _():
        gather(1, here.z // 4, 1)

    @pl.when(here.z % 4 == 3)
    def _():
        gather(2, here.z // 4, 2)

    dq_out.wait()
    dx_out.wait()
    for copy in sent:
        copy.wait_send()
    for t in range(4):
        for p in range(counts[groups[t]]):
            by, copy = z_copy(t, p)

            @pl.when(by != 0)
            def _():
                copy.wait_send()


PARTS = ((0, 0, 128), (0, 128, 128), (1, 0, 64), (1, 64, 64), (1, 128, 64), (1, 192, 64), (2, 0, 32), (3, 0, 32))


def hand_over(*refs):
    came, given, held, sems = refs[:4], refs[4:8], refs[8:12], refs[12]
    ins, outs = [], []
    for i, (which, at, rows) in enumerate(PARTS):
        part = pl.ds(at, rows)
        ins.append(
            pltpu.make_async_copy(came[which].at[part], held[which].at[part], sems.at[0, i])
        )
        outs.append(
            pltpu.make_async_copy(held[which].at[part], given[which].at[part], sems.at[1, i])
        )
    for copy in ins:
        copy.start()
    for copy, onward in zip(ins, outs):
        copy.wait()
        onward.start()
    for copy in outs:
        copy.wait()


def shards(
    inputs,
    query_rows,
    saved_key_rows,
    value_rows,
    grad_out,
    key_weight,
    value_weight,
    block_pairs,
    pair_counts,
):
    vmem = pl.BlockSpec(memory_space=pltpu.VMEM)
    smem = pl.BlockSpec(memory_space=pltpu.SMEM)
    anywhere = pl.BlockSpec(memory_space=pl.ANY)
    shapes = [
        jax.ShapeDtypeStruct((TOK, HD), BF),
        jax.ShapeDtypeStruct((TOK, D), BF),
        jax.ShapeDtypeStruct((32, TILE), F32),
        jax.ShapeDtypeStruct((32, TILE), F32),
    ]
    made = pl.pallas_call(
        whole_kernel,
        out_shape=shapes,
        in_specs=[anywhere] * 7 + [smem] * 2,
        out_specs=[anywhere] * 2 + [vmem] * 2,
        scratch_shapes=[
            pltpu.VMEM((TOK, HD), BF),
            pltpu.VMEM((TOK, HD), BF),
            pltpu.VMEM((TOK, HD), BF),
            pltpu.VMEM((TOK, HD), BF),
            pltpu.VMEM((TOK, HD), BF),
            pltpu.VMEM((TOK, D), BF),
            pltpu.VMEM((2, 512, BLK), F32),
            pltpu.VMEM((H, HALO, HS), BF),
            pltpu.VMEM((H, HALO, HS), BF),
            pltpu.VMEM((H, HALO, HS), BF),
            pltpu.VMEM((H, HALO, HS), BF),
            pltpu.VMEM((2, 2, TOK, HS), F32),
            pltpu.VMEM((H, 8, TOK), F32),
            pltpu.VMEM((H, 8, TOK), F32),
            pltpu.VMEM((H, 8, BLK), F32),
            pltpu.VMEM((NF, 2, TILE, HD), BF),
            pltpu.VMEM((2, TOK, HD), BF),
            [
                pltpu.VMEM((2, RING, 2, 128, TOK), BF),
                pltpu.VMEM((2, RING, 2, 64, TOK), BF),
                pltpu.VMEM((2, 2, RING, 64, TOK), BF),
            ],
            pltpu.VMEM((2, RING, TOK, TILE), BF),
            [
                [
                    pltpu.VMEM((4, height, TILE), BF),
                    pltpu.VMEM((4, height, TILE), BF),
                    pltpu.VMEM((2, 4, height, TILE), BF),
                    pltpu.VMEM((2, 4, height, TILE), BF),
                    pltpu.VMEM((height, TILE), BF),
                    pltpu.VMEM((2, height // 2, TILE), BF),
                    pltpu.VMEM((2, height, TILE), BF),
                    pltpu.VMEM((2, height, TILE), BF),
                    pltpu.VMEM((3, height, TILE), F32),
                ]
                for height in (256, 128, 64, 64)
            ],
            [pltpu.VMEM((count, 2, 32, TILE), F32) for count in (4, 2, 2)],
            [pltpu.VMEM((count, 2, 32, TILE), BF) for count in (4, 2, 2)],
            pltpu.VMEM((NZ, 2, 32, TILE), BF),
            pltpu.SemaphoreType.DMA((2, 4, H)),
            pltpu.SemaphoreType.DMA((2, 4, H)),
            pltpu.SemaphoreType.DMA((2, 2, H)),
            pltpu.SemaphoreType.DMA((2, 14)),
            pltpu.SemaphoreType.DMA((2, RING)),
            pltpu.SemaphoreType.DMA((2, H)),
            pltpu.SemaphoreType.DMA((2, 4, 12)),
            pltpu.SemaphoreType.DMA((2, 4, 6)),
            pltpu.SemaphoreType.DMA((4, 4)),
            pltpu.SemaphoreType.DMA((2, NZ)),
            pltpu.SemaphoreType.DMA((12,)),
        ],
        compiler_params=pltpu.CompilerParams(
            collective_id=0, has_side_effects=True, vmem_limit_bytes=56 * 1024 * 1024
        ),
    )(
        inputs[0],
        query_rows[0],
        saved_key_rows[0],
        value_rows[0],
        grad_out[0],
        key_weight,
        value_weight,
        block_pairs[0].T,
        pair_counts,
    )
    grad_query, input_gradient, key_total, value_total = pl.pallas_call(
        hand_over,
        out_shape=shapes,
        in_specs=[anywhere] * 4,
        out_specs=[anywhere] * 4,
        scratch_shapes=[pltpu.VMEM(shape.shape, shape.dtype) for shape in shapes]
        + [pltpu.SemaphoreType.DMA((2, len(PARTS)))],
    )(*made)
    return (grad_query[None], input_gradient[None], key_total.T, value_total.T)


def solution(mesh):
    return jax.shard_map(
        shards,
        mesh=mesh,
        in_specs=(
            P("fsdp", "tm", None),
            P("fsdp", "tm", None),
            P("fsdp", "tm", None),
            P("fsdp", "tm", None),
            P("fsdp", "tm", None),
            P("fsdp", None),
            P("fsdp", None),
            P("tm", None, None),
            P("tm"),
        ),
        out_specs=(P("fsdp", "tm", None), P("fsdp", "tm", None), P("fsdp", "tm"), P("fsdp", "tm")),
        check_vma=False,
    )
```

```python
import jax
import jax.numpy as jnp
from jax import lax
from jax.experimental import pallas as pl
from jax.experimental.pallas import tpu as pltpu
from jax.sharding import PartitionSpec as P

H = 8
HS = 128
BLK = 128
TOK = 256
HD = 1024
D = 2048
MAXP = 8
BF = jnp.bfloat16
F32 = jnp.float32
MESH = pl.DeviceIdType.MESH
RING = 4
NZ = 8
NTM = RING * NZ
NF = 8
TILE = 256
AHEAD = 3
HALO = 384
SCALE = HS**-0.5
NN = (((1,), (0,)), ((), ()))
NT = (((1,), (1,)), ((), ()))
TN = (((0,), (0,)), ((), ()))


def mm(a, b, dims):
    return lax.dot_general(a, b, dims, preferred_element_type=F32)


class Place:
    def __init__(self):
        self.tm = lax.axis_index("tm")
        self.fsdp = lax.axis_index("fsdp")
        self.z, self.y = self.tm // RING, self.tm % RING
        self.x, self.core = self.fsdp // 2, self.fsdp % 2

    def at(self, x=None, core=None, z=None, y=None):
        x = self.x if x is None else x
        core = self.core if core is None else core
        z = self.z if z is None else z
        y = self.y if y is None else y
        return (z * RING + y, x * 2 + core)

    def step(self, axis, by):
        if axis == "x":
            return self.at(x=(self.x + by) % RING)
        if axis == "y":
            return self.at(y=(self.y + by) % RING)
        return self.at(z=(self.z + by) % NZ)

    def partner(self):
        return self.at(core=1 - self.core)

    def later(self, by):
        return ((self.tm + NTM + by) % NTM, self.fsdp)


def greet(devices):
    barrier = pltpu.get_barrier_semaphore()
    for device in devices:
        pl.semaphore_signal(barrier, inc=1, device_id=device, device_id_type=MESH)
    pl.semaphore_wait(barrier, len(devices))


def whole_kernel(
    x_hbm,
    q_hbm,
    k_hbm,
    v_hbm,
    do_hbm,
    wk_hbm,
    wv_hbm,
    pairs_ref,
    count_ref,
    dq_hbm,
    dx_hbm,
    key_ref,
    value_ref,
    q_ref,
    k_ref,
    v_ref,
    do_ref,
    dq,
    dx,
    bias,
    kwin,
    vwin,
    qwin,
    cwin,
    own,
    stat_send,
    stat_near,
    stat_far,
    wbuf,
    g,
    gts,
    xs,
    rings,
    finals,
    z_sends,
    z_recv,
    halo_sems,
    relay_sems,
    stat_sems,
    w_sems,
    x_sems,
    gt_sems,
    ring_sems,
    ring2_sems,
    z_sent,
    z_came,
    local_sems,
):
    here = Place()
    later, earlier, partner = here.later(1), here.later(-1), here.partner()
    earlier2 = here.later(-2)

    loads = [
        pltpu.make_async_copy(src, dst, local_sems.at[i])
        for i, (src, dst) in enumerate(
            ((k_hbm, k_ref), (q_hbm, q_ref), (v_hbm, v_ref), (do_hbm, do_ref))
        )
    ]
    own_rows = []
    for i, src in enumerate((wk_hbm, wv_hbm)):
        own_rows.append(pltpu.make_async_copy(src, wbuf.at[here.fsdp, i], local_sems.at[4 + i]))
    for xp in range(RING):
        columns = pl.ds(pl.multiple_of(xp * 512 + here.core * TILE, TILE), TILE)
        own_rows.append(pltpu.make_async_copy(x_hbm.at[:, columns], xs.at[0, xp], local_sems.at[6 + xp]))
    for copy in loads + own_rows:
        copy.start()

    greet(
        [partner, later, earlier, here.later(2), earlier2]
        + [here.step(axis, by) for axis in ("x", "y") for by in (1, 3)]
        + [here.step("x", 2), here.step("y", 2)]
        + [here.step("z", by) for by in range(1, NZ)]
    )
    sent = []

    def remote(src, dst, sems, at, device):
        return pltpu.make_async_remote_copy(
            src_ref=src,
            dst_ref=dst,
            send_sem=sems.at[(0,) + at],
            recv_sem=sems.at[(1,) + at],
            device_id=device,
            device_id_type=MESH,
        )

    def send(src, dst, sems, at, device):
        copy = remote(src, dst, sems, at, device)
        copy.start()
        sent.append(copy)
        return copy

    def lanes(h):
        head = h // 4 + 4 * (h % 2) + 2 * ((h % 4) // 2)
        return pl.ds(pl.multiple_of(head * HS, HS), HS)

    streams = (
        (k_hbm, kwin, BLK, 2 * BLK, 0, later),
        (v_hbm, vwin, BLK, 2 * BLK, 0, later),
        (q_hbm, qwin, 0, 0, 2 * BLK, earlier),
        (do_hbm, cwin, 0, 0, 2 * BLK, earlier),
    )

    def halo(h):
        return [
            remote(ref.at[:, lanes(h)], win.at[h, pl.ds(at, TOK)], halo_sems, (i, h), device)
            for i, (ref, win, at, _, _, device) in enumerate(streams)
        ]

    def relay(h, which=range(4)):
        copies = []
        for i in which:
            _, win, _, src, dst, device = streams[i]
            copies.append(
                remote(win.at[h, pl.ds(src, BLK)], win.at[h, pl.ds(dst, BLK)], relay_sems, (i, h), device)
            )
        return copies

    def stats(h):
        return [
            remote(stat_send.at[h], stat_near.at[h], stat_sems, (0, h), earlier),
            remote(stat_send.at[h, :, pl.ds(0, BLK)], stat_far.at[h], stat_sems, (1, h), earlier2),
        ]

    starts = (0, 4, 6)

    def turned(h, group):
        rows = pl.ds(pl.multiple_of((h - starts[group]) * 32, 32), 32)
        gt = gts[group]
        return remote(gt.at[0, :, :, rows], gt.at[1, :, :, rows], gt_sems, (h,), partner)

    def start(copies):
        for copy in copies:
            copy.start()

    def arrive(copies):
        for copy in copies:
            copy.wait_recv()

    for h in range(AHEAD):
        start(halo(h))

    weights = (wk_hbm, wv_hbm)
    right, left = here.step("x", 1), here.step("x", 3)
    mine = here.fsdp
    left_id = ((here.x + 3) % RING) * 2 + here.core
    right_id = ((here.x + 1) % RING) * 2 + here.core
    opp_id = ((here.x + 2) % RING) * 2 + here.core
    from_left, from_right = {}, {}
    for i in (0, 1):
        from_left[i] = send(weights[i], wbuf.at[mine, i], w_sems, (i,), right)
        from_right[1 - i] = send(weights[1 - i], wbuf.at[mine, 1 - i], w_sems, (2 + 1 - i,), left)
    crossed = []
    for i in (0, 1):
        crossed.append(send(weights[i], wbuf.at[mine, i], w_sems, (6 + i,), partner))
    x_cross = []
    for xp in range(RING):
        theirs = pl.multiple_of(xp * 512 + (1 - here.core) * TILE, TILE)
        x_cross.append(send(x_hbm.at[:, pl.ds(theirs, TILE)], xs.at[1, xp], x_sems, (xp,), partner))

    def forward_weights():
        from_left[0].wait_recv()
        opp_k = send(wbuf.at[left_id, 0], wbuf.at[left_id, 0], w_sems, (4,), right)
        crossed.append(send(wbuf.at[left_id, 0], wbuf.at[left_id, 0], w_sems, (8,), partner))
        from_right[1].wait_recv()
        opp_v = send(wbuf.at[right_id, 1], wbuf.at[right_id, 1], w_sems, (5,), left)
        crossed.append(send(wbuf.at[right_id, 1], wbuf.at[right_id, 1], w_sems, (9,), partner))
        return opp_k, opp_v

    def cross_weights(opp_k, opp_v):
        from_left[1].wait_recv()
        crossed.append(send(wbuf.at[left_id, 1], wbuf.at[left_id, 1], w_sems, (10,), partner))
        from_right[0].wait_recv()
        crossed.append(send(wbuf.at[right_id, 0], wbuf.at[right_id, 0], w_sems, (11,), partner))
        opp_k.wait_recv()
        crossed.append(send(wbuf.at[opp_id, 0], wbuf.at[opp_id, 0], w_sems, (12,), partner))
        opp_v.wait_recv()
        crossed.append(send(wbuf.at[opp_id, 1], wbuf.at[opp_id, 1], w_sems, (13,), partner))

    key_at = lax.broadcasted_iota(jnp.int32, (BLK, BLK), 0)
    query_at = lax.broadcasted_iota(jnp.int32, (BLK, BLK), 1)
    levels = {}
    for qb in range(2):
        for kb in range(4):
            query_block = here.tm * 2 + qb
            key_block = query_block - 3 + kb
            hit = None
            for r in range(MAXP):
                same = (
                    (r < count_ref[0])
                    & (pairs_ref[0, r] == query_block)
                    & (pairs_ref[1, r] == key_block)
                )
                hit = same if hit is None else hit | same
            levels[qb, kb] = jnp.where(hit, 0.0, -jnp.inf)
            level = jnp.full((BLK, BLK), levels[qb, kb], F32)
            if kb == 3:
                level = jnp.where(key_at <= query_at, level, -jnp.inf)
            bias[qb, kb * BLK : (kb + 1) * BLK] = level
    rows = [
        jnp.concatenate([jnp.full((1, BLK), levels[0, a], F32), jnp.full((1, BLK), levels[1, b], F32)], axis=1)
        for a, b in ((1, 0), (2, 1), (0, 0))
    ]
    for h in range(H):
        for i, row in enumerate(rows):
            stat_send[h, 3 + i : 4 + i] = row

    def query_side(h):
        query, cotangent = q_ref[:, lanes(h)], do_ref[:, lanes(h)]
        keys = jnp.concatenate([kwin[h], k_ref[:, lanes(h)]], axis=0)
        values = jnp.concatenate([vwin[h], v_ref[:, lanes(h)]], axis=0)
        scores = mm(keys, query, NT)
        grad_probs = mm(values, cotangent, NT)
        probs_parts, grads_parts, noted = [], [], []
        for qb in range(2):
            near, columns = slice(qb * BLK, qb * BLK + 512), slice(qb * BLK, qb * BLK + BLK)
            score = scores[near, columns] * SCALE + bias[qb]
            most = jnp.max(score, axis=0, keepdims=True)
            prob = jnp.exp(score - most)
            share = 1.0 / jnp.sum(prob, axis=0, keepdims=True)
            prob = prob * share
            low = prob.astype(BF)
            grad = grad_probs[near, columns]
            row_dot = jnp.sum(low.astype(F32) * grad, axis=0, keepdims=True)
            probs_parts.append(low)
            grads_parts.append((prob * (grad - row_dot)).astype(BF))
            noted.append((most, share, row_dot))
        for i in range(3):
            stat_send[h, i : i + 1] = jnp.concatenate([noted[0][i], noted[1][i]], axis=1)
        start(stats(h))
        blank = jnp.zeros((BLK, BLK), BF)
        grads_low = jnp.concatenate(
            [
                jnp.concatenate([grads_parts[0], blank], axis=0),
                jnp.concatenate([blank, grads_parts[1]], axis=0),
            ],
            axis=1,
        )
        probs_own = jnp.concatenate(
            [jnp.concatenate([probs_parts[0][HALO:], blank], axis=0), probs_parts[1][2 * BLK :]],
            axis=1,
        )
        dq[:, lanes(h)] = (mm(grads_low, keys, TN) * SCALE).astype(BF)
        own[h % 2, 0] = mm(grads_low[HALO:], query, NN)
        own[h % 2, 1] = mm(probs_own, cotangent, NN)

    def key_side(h, group):
        arrive(relay(h, (2, 3)) + stats(h))
        query, cotangent = qwin[h], cwin[h]
        keys, values = k_ref[:, lanes(h)], v_ref[:, lanes(h)]
        scores = mm(keys, query, NT)
        grad_probs = mm(values, cotangent, NT)
        most, share, row_dot = (
            jnp.concatenate([stat_near[h, i : i + 1], stat_far[h, i : i + 1]], axis=1) for i in range(3)
        )
        never = jnp.full((1, BLK), -jnp.inf, F32)
        levels = (
            jnp.concatenate([stat_near[h, 3:4], never], axis=1),
            jnp.concatenate([stat_near[h, 4:5], stat_far[h, 5:6]], axis=1),
        )
        probs_parts, grads_parts = [], []
        for b in range(2):
            block = slice(b * BLK, b * BLK + BLK)
            prob = jnp.exp(scores[block] * SCALE + levels[b] - most) * share
            probs_parts.append(prob.astype(BF))
            grads_parts.append((prob * (grad_probs[block] - row_dot)).astype(BF))
        keys_grad = mm(jnp.concatenate(grads_parts, axis=0), query, NN)
        values_grad = mm(jnp.concatenate(probs_parts, axis=0), cotangent, NN)
        for i, full in enumerate(((own[h % 2, 0] + keys_grad) * SCALE, own[h % 2, 1] + values_grad)):
            low = full.astype(BF)
            g[i, :, lanes(h)] = low
            flipped = low.T
            rows = pl.ds(pl.multiple_of((h - starts[group]) * 32, 32), 32)
            for yp in range(RING):
                part = flipped[yp * 32 : yp * 32 + 32]
                if group == 2:
                    gts[2][0, i, yp, rows] = part
                else:
                    gts[group][0, yp, i, rows] = part
        turned(h, group).start()

    def pass_on(h):
        for near, onward in zip(halo(h), relay(h)):
            near.wait_recv()
            onward.start()

    for copy in loads:
        copy.wait()
    pass_on(0)

    axes = (("x", "y"), ("y", "x"), ("x", "y"), ("y", "x"))
    groups = (0, 1, 2, 2)
    heights = (256, 128, 64, 64)
    place = {"x": here.x, "y": here.y}
    slots = (2, 1, 3, 0)
    ways = (1, 3)
    opposite, beside, second, pieces = {}, {}, {}, {}

    def block(t, ring, slot):
        b = (place[axes[t][1]] + slots[slot]) % RING
        xp, yp = (b, ring) if axes[t][0] == "y" else (ring, b)
        terms = []
        for side in range(2):
            if t < 2:
                lhs = gts[t][side, yp].reshape(heights[t], TOK)
            else:
                lhs = gts[2][side, t - 2, yp]
            terms.append(mm(lhs, xs[side, xp], NN))
        return terms[0] + terms[1]

    def ring(t, d):
        return (place[axes[t][0]] + ways[d]) % RING

    def send_opposite(t):
        opp_send, opp_recv = rings[t][:2]
        opp = (place[axes[t][0]] + 2) % RING
        for i in range(2):
            for d in range(2):
                slot = 2 * d + i
                opp_send[slot] = block(t, opp, slot).astype(BF)
                opposite[t, slot] = send(
                    opp_send.at[slot],
                    opp_recv.at[slot],
                    ring_sems,
                    (t, slot),
                    here.step(axes[t][0], ways[d]),
                )

    def give(t, d, slot, value):
        nb_send, nb_recv = rings[t][2:4]
        nb_send[d, slot] = value.astype(BF)
        beside[t, d, slot] = send(
            nb_send.at[d, slot],
            nb_recv.at[d, slot],
            ring_sems,
            (t, 4 + d * 4 + slot),
            here.step(axes[t][0], ways[d]),
        )

    def send_free(t):
        for i in range(2):
            for d in range(2):
                slot = 2 * (1 - d) + i
                give(t, d, slot, block(t, ring(t, d), slot))

    def send_bound(t):
        opp_recv = rings[t][1]
        order = [(d, 2 * d + i) for i in range(2) for d in range(2)]
        made = [block(t, ring(t, d), slot) for d, slot in order]
        for (d, slot), value in zip(order, made):
            opposite[t, slot].wait_recv()
            give(t, d, slot, value + opp_recv[slot].astype(F32))

    def total(t, slot, value):
        nb_recv = rings[t][3]
        for d in range(2):
            beside[t, d, slot].wait_recv()
        return value + nb_recv[0, slot].astype(F32) + nb_recv[1, slot].astype(F32)

    def give2(t, d, half, value):
        nb2_send, nb2_recv = rings[t][6:8]
        height = heights[t] // 2
        part = pl.ds(height * half, height)
        nb2_send[d, part] = value.astype(BF)
        pieces[t, d, half] = send(
            nb2_send.at[d, part],
            nb2_recv.at[d, part],
            ring2_sems,
            (t, 2 + 2 * d + half),
            here.step(axes[t][1], ways[d]),
        )

    def open_second(t):
        opp2_send, opp2_recv = rings[t][4:6]
        sums = rings[t][8]
        height = heights[t] // 2
        made = [block(t, place[axes[t][0]], slot) for slot in range(4)]
        opp2_send[...] = total(t, 0, made[0]).astype(BF)
        for d in range(2):
            second[t, d] = send(
                opp2_send.at[pl.ds(height * d, height)],
                opp2_recv.at[d],
                ring2_sems,
                (t, d),
                here.step(axes[t][1], 2 if t > 1 else ways[d]),
            )
        for d in range(2):
            sums[d] = total(t, 1 + d, made[1 + d])
            give2(t, d, 1 - d, sums[d, pl.ds(height * (1 - d), height)])
            if t > 1:
                give2(t, d, d, sums[d, pl.ds(height * d, height)])
        sums[2] = total(t, 3, made[3])

    def bound_second(t):
        opp2_recv, sums = rings[t][5], rings[t][8]
        height = heights[t] // 2
        for d in range(2):
            second[t, d].wait_recv()
            give2(t, d, d, sums[d, pl.ds(height * d, height)] + opp2_recv[d].astype(F32))

    def owner(t, p):
        return (4 * (p % 2) + 2 * (p // 2), 1 + 4 * p, 3 + 4 * p)[groups[t]]

    def z_copy(t, p):
        by = (owner(t, p) - here.z + NZ) % NZ
        at, there = (p,), (by,)
        if t > 1:
            at, there = at + (t - 2,), there + (t - 2,)
        copy = pltpu.make_async_remote_copy(
            src_ref=z_sends[groups[t]].at[at],
            dst_ref=z_recv.at[there],
            send_sem=z_sent.at[t, p],
            recv_sem=z_came.at[max(t - 2, 0), by],
            device_id=here.at(z=owner(t, p)),
            device_id_type=MESH,
        )
        return by, copy

    counts = (4, 2, 2)

    def finish(t):
        nb2_recv, sums = rings[t][7], rings[t][8]
        for d in range(2):
            for half in range(2):
                pieces[t, d, half].wait_recv()
        whole = sums[2] + nb2_recv[0].astype(F32) + nb2_recv[1].astype(F32)
        if t > 1:
            for d in range(2):
                second[t, d].wait_recv()
            whole = whole + rings[t][5][...].reshape(heights[t], TILE).astype(F32)
        count = counts[groups[t]]
        for i, half in enumerate((0, 1) if t < 2 else (t - 2,)):
            for p in range(count):
                part = whole[(i * count + p) * 32 : (i * count + p) * 32 + 32]
                finals[groups[t]][p, half] = part
                z_sends[groups[t]][p, half] = part.astype(BF)
        for p in range(count):
            by, copy = z_copy(t, p)

            @pl.when(by != 0)
            def _():
                copy.start()

    def input_rows(f, carry):
        columns = pl.ds(pl.multiple_of(f * TILE, TILE), TILE)
        dx[:, columns] = (mm(g[0], wbuf[f, 0], NT) + mm(g[1], wbuf[f, 1], NT)).astype(BF)
        return carry

    def body(h, carry, group=0, first=False, more=True, last=False, before=None):
        if more:
            start(halo(h + AHEAD))
        if not last:
            pass_on(h + 1)
        if before is not None:
            before()
        arrive(relay(h, (0, 1)))
        query_side(h)
        if not first:
            key_side(h - 1, group)
        return carry

    body(0, 0, first=True)
    lax.fori_loop(1, 3, body, 0)
    opp_weights = forward_weights()
    body(3, 0)
    body(4, 0)

    def open_first():
        for copy in own_rows:
            copy.wait()
        arrive(x_cross + [turned(h, 0) for h in range(4)])
        send_opposite(0)

    def open_next():
        send_bound(0)
        arrive([turned(h, 1) for h in (4, 5)])
        send_opposite(1)

    body(5, 0, group=1, more=False, before=open_first)
    body(6, 0, group=1, more=False, before=lambda: send_free(0))
    body(7, 0, group=2, more=False, last=True, before=open_next)
    send_free(1)
    key_side(7, 2)
    dq_out = pltpu.make_async_copy(dq, dq_hbm, local_sems.at[10])
    dq_out.start()
    send_bound(1)
    arrive([turned(h, 2) for h in (6, 7)])
    for t in (2, 3):
        send_opposite(t)
    for t in (2, 3):
        send_free(t)
    open_second(0)
    for t in (2, 3):
        send_bound(t)
    bound_second(0)
    cross_weights(*opp_weights)
    open_second(1)
    finish(0)
    arrive(crossed)
    lax.fori_loop(0, 1, input_rows, 0)
    for t in (2, 3):
        open_second(t)
    bound_second(1)
    lax.fori_loop(1, 3, input_rows, 0)
    finish(1)
    lax.fori_loop(3, 5, input_rows, 0)
    for t in (2, 3):
        finish(t)
    lax.fori_loop(5, NF, input_rows, 0)
    dx_out = pltpu.make_async_copy(dx, dx_hbm, local_sems.at[11])
    dx_out.start()
    def drain(h, carry):
        for copy in halo(h) + relay(h) + stats(h):
            copy.wait_send()
        return carry

    lax.fori_loop(0, H, drain, 0)
    for h in range(H):
        turned(h, (h > 3) + (h > 5)).wait_send()
    for copy in sent:
        copy.wait_send()
    sent.clear()

    def gather(group, p, halves):
        for half in range(halves):
            for by in range(1, NZ):
                at, there = ((p,), (by,)) if halves == 1 else ((p, half), (by, half))
                pltpu.make_async_remote_copy(
                    src_ref=z_sends[group].at[at],
                    dst_ref=z_recv.at[there],
                    send_sem=z_sent.at[0, 0],
                    recv_sem=z_came.at[half, by],
                    device_id=here.step("z", by),
                    device_id_type=MESH,
                ).wait_recv()
        for half, out_ref in enumerate((key_ref, value_ref)):
            whole = finals[group][p, half]
            for by in range(1, NZ):
                whole = whole + z_recv[by, half].astype(F32)
            out_ref[...] = whole

    @pl.when(here.z % 2 == 0)
    def _():
        gather(0, here.z // 4 + 2 * ((here.z % 4) // 2), 1)

    @pl.when(here.z % 4 == 1)
    def _():
        gather(1, here.z // 4, 1)

    @pl.when(here.z % 4 == 3)
    def _():
        gather(2, here.z // 4, 2)

    dq_out.wait()
    dx_out.wait()
    for copy in sent:
        copy.wait_send()
    for t in range(4):
        for p in range(counts[groups[t]]):
            by, copy = z_copy(t, p)

            @pl.when(by != 0)
            def _():
                copy.wait_send()


PARTS = ((0, 0, 128), (0, 128, 128), (1, 0, 64), (1, 64, 64), (1, 128, 64), (1, 192, 64), (2, 0, 32), (3, 0, 32))


def hand_over(*refs):
    came, given, held, sems = refs[:4], refs[4:8], refs[8:12], refs[12]
    ins, outs = [], []
    for i, (which, at, rows) in enumerate(PARTS):
        part = pl.ds(at, rows)
        ins.append(
            pltpu.make_async_copy(came[which].at[part], held[which].at[part], sems.at[0, i])
        )
        outs.append(
            pltpu.make_async_copy(held[which].at[part], given[which].at[part], sems.at[1, i])
        )
    for copy in ins:
        copy.start()
    for copy, onward in zip(ins, outs):
        copy.wait()
        onward.start()
    for copy in outs:
        copy.wait()


def shards(
    inputs,
    query_rows,
    saved_key_rows,
    value_rows,
    grad_out,
    key_weight,
    value_weight,
    block_pairs,
    pair_counts,
):
    vmem = pl.BlockSpec(memory_space=pltpu.VMEM)
    smem = pl.BlockSpec(memory_space=pltpu.SMEM)
    anywhere = pl.BlockSpec(memory_space=pl.ANY)
    shapes = [
        jax.ShapeDtypeStruct((TOK, HD), BF),
        jax.ShapeDtypeStruct((TOK, D), BF),
        jax.ShapeDtypeStruct((32, TILE), F32),
        jax.ShapeDtypeStruct((32, TILE), F32),
    ]
    made = pl.pallas_call(
        whole_kernel,
        out_shape=shapes,
        in_specs=[anywhere] * 7 + [smem] * 2,
        out_specs=[anywhere] * 2 + [vmem] * 2,
        scratch_shapes=[
            pltpu.VMEM((TOK, HD), BF),
            pltpu.VMEM((TOK, HD), BF),
            pltpu.VMEM((TOK, HD), BF),
            pltpu.VMEM((TOK, HD), BF),
            pltpu.VMEM((TOK, HD), BF),
            pltpu.VMEM((TOK, D), BF),
            pltpu.VMEM((2, 512, BLK), F32),
            pltpu.VMEM((H, HALO, HS), BF),
            pltpu.VMEM((H, HALO, HS), BF),
            pltpu.VMEM((H, HALO, HS), BF),
            pltpu.VMEM((H, HALO, HS), BF),
            pltpu.VMEM((2, 2, TOK, HS), F32),
            pltpu.VMEM((H, 8, TOK), F32),
            pltpu.VMEM((H, 8, TOK), F32),
            pltpu.VMEM((H, 8, BLK), F32),
            pltpu.VMEM((NF, 2, TILE, HD), BF),
            pltpu.VMEM((2, TOK, HD), BF),
            [
                pltpu.VMEM((2, RING, 2, 128, TOK), BF),
                pltpu.VMEM((2, RING, 2, 64, TOK), BF),
                pltpu.VMEM((2, 2, RING, 64, TOK), BF),
            ],
            pltpu.VMEM((2, RING, TOK, TILE), BF),
            [
                [
                    pltpu.VMEM((4, height, TILE), BF),
                    pltpu.VMEM((4, height, TILE), BF),
                    pltpu.VMEM((2, 4, height, TILE), BF),
                    pltpu.VMEM((2, 4, height, TILE), BF),
                    pltpu.VMEM((height, TILE), BF),
                    pltpu.VMEM((2, height // 2, TILE), BF),
                    pltpu.VMEM((2, height, TILE), BF),
                    pltpu.VMEM((2, height, TILE), BF),
                    pltpu.VMEM((3, height, TILE), F32),
                ]
                for height in (256, 128, 64, 64)
            ],
            [pltpu.VMEM((count, 2, 32, TILE), F32) for count in (4, 2, 2)],
            [pltpu.VMEM((count, 2, 32, TILE), BF) for count in (4, 2, 2)],
            pltpu.VMEM((NZ, 2, 32, TILE), BF),
            pltpu.SemaphoreType.DMA((2, 4, H)),
            pltpu.SemaphoreType.DMA((2, 4, H)),
            pltpu.SemaphoreType.DMA((2, 2, H)),
            pltpu.SemaphoreType.DMA((2, 14)),
            pltpu.SemaphoreType.DMA((2, RING)),
            pltpu.SemaphoreType.DMA((2, H)),
            pltpu.SemaphoreType.DMA((2, 4, 12)),
            pltpu.SemaphoreType.DMA((2, 4, 6)),
            pltpu.SemaphoreType.DMA((4, 4)),
            pltpu.SemaphoreType.DMA((2, NZ)),
            pltpu.SemaphoreType.DMA((12,)),
        ],
        compiler_params=pltpu.CompilerParams(
            collective_id=0, has_side_effects=True, vmem_limit_bytes=56 * 1024 * 1024
        ),
    )(
        inputs[0],
        query_rows[0],
        saved_key_rows[0],
        value_rows[0],
        grad_out[0],
        key_weight,
        value_weight,
        block_pairs[0].T,
        pair_counts,
    )
    grad_query, input_gradient, key_total, value_total = pl.pallas_call(
        hand_over,
        out_shape=shapes,
        in_specs=[anywhere] * 4,
        out_specs=[anywhere] * 4,
        scratch_shapes=[pltpu.VMEM(shape.shape, shape.dtype) for shape in shapes]
        + [pltpu.SemaphoreType.DMA((2, len(PARTS)))],
    )(*made)
    return (grad_query[None], input_gradient[None], key_total.T, value_total.T)


def solution(mesh):
    return jax.shard_map(
        shards,
        mesh=mesh,
        in_specs=(
            P("fsdp", "tm", None),
            P("fsdp", "tm", None),
            P("fsdp", "tm", None),
            P("fsdp", "tm", None),
            P("fsdp", "tm", None),
            P("fsdp", None),
            P("fsdp", None),
            P("tm", None, None),
            P("tm"),
        ),
        out_specs=(P("fsdp", "tm", None), P("fsdp", "tm", None), P("fsdp", "tm"), P("fsdp", "tm")),
        check_vma=False,
    )
```
